512 devices in a mesh: row: 16 (over z, core), head: 32 (over y, x).
Axes of the slice: x: 4, y: 8, z: 8, core: 2. Of those that a mesh axis runs over, the one named last changes fastest.
Arguments:
- hidden: bfloat16 [32, 8192], P(None, 'row'), may hold values from -12 to 12
- norm_gain: bfloat16 [8192], P('row'), may hold values from 0.5 to 1.5
- input_weight: bfloat16 [8192, 2, 16384], P('row', None, 'head'), may hold values from -0.0625 to 0.0625
- group_weight: bfloat16 [8192, 4096], P('row', 'head'), may hold values from -0.0625 to 0.0625
- step_weight: bfloat16 [8192, 256], P('row', 'head'), may hold values from -0.0625 to 0.0625
- conv_inner_weight: bfloat16 [4, 16384], P(None, 'head'), may hold values from -3 to 3
- conv_group_weight: bfloat16 [4, 4096], P(None, 'head'), may hold values from -3 to 3
- conv_inner_state: bfloat16 [32, 3, 16384], P('row', None, 'head'), may hold values from -6 to 6
- conv_group_state: bfloat16 [32, 3, 4096], P('row', None, 'head'), may hold values from -6 to 6
- timestep_bias: float32 [256], P('head'), may hold values from -3 to 0.5
- decay_log: float32 [256], P('head'), may hold values from -1 to 2
- skip_gain: float32 [256], P('head'), may hold values from 0.5 to 1.5
- recurrent_state: bfloat16 [32, 256, 64, 256], P('row', 'head'), may hold values from -6 to 6
- mixer_gain: bfloat16 [16384], P('head'), may hold values from 0.5 to 1.5
- output_weight: bfloat16 [16384, 8192], P('head', 'row'), may hold values from -0.046875 to 0.046875
- final_gain: bfloat16 [8192], P('row'), may hold values from 0.5 to 1.5
- lexicon_matrix: bfloat16 [8192, 65536], P('row', 'head'), may hold values from -0.4375 to 0.4375
- token_mask: int32 [32, 65536], P('row', 'head'), may hold values 0 or 1
- min_share: int32 [32], P('row'), may hold values from 1311 to 13107
Outputs:
- next_state: bfloat16 [32, 256, 64, 256], P('row', 'head')
- next_conv_inner: bfloat16 [32, 3, 16384], P('row', None, 'head')
- next_conv_group: bfloat16 [32, 3, 4096], P('row', None, 'head')
- layer_out: bfloat16 [32, 8192], P(None, 'row')
- next_probs: bfloat16 [32, 65536], P('row', 'head')
The draws below stay inside these ranges and needn't reach their ends.
Inputs may be any that keep to these rules, and one draw needn't show every extreme that they name: `min_share`: the smallest share of the row's top probability that a token keeps in full at twice that share, times 65536.
All inputs are finite; a program needn't handle non-finite values. No bound on the sum of `token_mask` on one device may be relied on, other than what follows from the above.
Results may differ from the reference program's by a relative error of at most 0.04.
Values may be sent and summed in bfloat16 or wider, within the bound.
A program may use at most 64 MiB of HBM per device.

```python
import math
import jax
import jax.numpy as jnp
from jax import lax

D = 8192
HEADS = 256
HEAD_DIM = 64
STATE = 256
GROUPS = 8
VOCAB = 65536
CONV = 4
ROWS = 32


def draw_hidden(key, part):
    key_list = jax.random.split(jax.random.fold_in(key, 17), 3)
    base_draw = jax.random.normal(key_list[0], (ROWS, D), jnp.float32)
    row_scale = jnp.exp(jax.random.uniform(key_list[1], (ROWS, 1), jnp.float32, math.log(0.3), math.log(3.0)))
    column_ramp = jnp.exp(math.log(3.0) * jnp.arange(D, dtype=jnp.float32)[None, :] / D)
    column_scale = 0.6 * column_ramp * jnp.exp(jax.random.uniform(key_list[2], (1, D), jnp.float32, -0.7, 0.7))
    return jnp.clip(base_draw * row_scale * column_scale, -12.0, 12.0).astype(jnp.bfloat16)


def plant(values, key, least, largest):
    place = [jax.random.randint(jax.random.fold_in(key, axis), (), 0, length) for axis, length in enumerate(values.shape)]
    longest = values.shape.index(max(values.shape))
    next_to = place[:longest] + [(place[longest] + 1) % values.shape[longest]] + place[longest + 1:]
    return values.at[tuple(place)].set(least).at[tuple(next_to)].set(largest)


def levels(own_key, shape, cuts, smallest, high):
    loudness = 1.0
    for axis_at, parts in cuts:
        heights = jax.random.uniform(jax.random.fold_in(jax.random.fold_in(own_key, 6), axis_at), (parts,), jnp.float32, smallest / len(cuts), high / len(cuts))
        loudness = loudness * jnp.repeat(jnp.exp(heights), shape[axis_at] // parts).reshape((-1,) + (1,) * (len(shape) - 1 - axis_at))
    return loudness


def centred(own_key, dims, spread, limit, cuts=(), kind=jnp.bfloat16):
    array = spread * jax.random.normal(own_key, dims, jnp.float32)
    if cuts:
        array = array * levels(own_key, dims, cuts, -0.22, 0.18)
    return jnp.clip(array, -limit, limit).astype(kind)


def setup_inputs(seed: int = 0) -> dict:
    keys = jax.random.split(jax.random.key(seed), 20)
    return {
        "hidden": draw_hidden(jax.random.fold_in(keys[19], 71), 0),
        "norm_gain": jnp.clip(1.0 + 0.1 * jax.random.normal(keys[1], (D,), jnp.float32), 0.5, 1.5).astype(jnp.bfloat16),
        "input_weight": centred(keys[2], (D, 2, HEADS * HEAD_DIM), D ** -0.5, 0.0625, ((0, 16), (2, 32))),
        "group_weight": centred(keys[3], (D, GROUPS * 2 * STATE), D ** -0.5, 0.0625, ((0, 16), (1, 32))),
        "step_weight": centred(keys[4], (D, HEADS), D ** -0.5, 0.0625, ((0, 16), (1, 32))),
        "conv_inner_weight": centred(keys[5], (CONV, HEADS * HEAD_DIM), 0.5, 3.0, ((1, 32),)),
        "conv_group_weight": centred(keys[6], (CONV, GROUPS * 2 * STATE), 0.5, 3.0, ((1, 32),)),
        "conv_inner_state": centred(keys[7], (ROWS, CONV - 1, HEADS * HEAD_DIM), 1.0, 6.0, ((0, 16), (2, 32))),
        "conv_group_state": centred(keys[8], (ROWS, CONV - 1, GROUPS * 2 * STATE), 1.0, 6.0, ((0, 16), (2, 32))),
        "timestep_bias": jnp.clip(-3.0 + 3.5 * jax.random.uniform(keys[9], (HEADS,), jnp.float32) ** levels(keys[9], (HEADS,), ((0, 32),), -0.2, 0.2), -3.0, 0.5),
        "decay_log": jnp.clip(-1.0 + 3.0 * jax.random.uniform(keys[10], (HEADS,), jnp.float32) ** levels(keys[10], (HEADS,), ((0, 32),), -0.2, 0.2), -1.0, 2.0),
        "skip_gain": jnp.clip(0.5 + 1.0 * jax.random.uniform(keys[11], (HEADS,), jnp.float32) ** levels(keys[11], (HEADS,), ((0, 32),), -0.2, 0.2), 0.5, 1.5),
        "recurrent_state": centred(keys[12], (ROWS, HEADS, HEAD_DIM, STATE), 1.0, 6.0, ((0, 16), (1, 32))),
        "mixer_gain": jnp.clip(1.0 + 0.1 * jax.random.normal(keys[13], (HEADS * HEAD_DIM,), jnp.float32), 0.5, 1.5).astype(jnp.bfloat16),
        "output_weight": centred(keys[14], (HEADS * HEAD_DIM, D), (HEADS * HEAD_DIM) ** -0.5, 0.046875, ((0, 32), (1, 16))),
        "final_gain": jnp.clip(1.0 + 0.1 * jax.random.normal(keys[15], (D,), jnp.float32), 0.5, 1.5).astype(jnp.bfloat16),
        "lexicon_matrix": centred(keys[16], (D, VOCAB), (2.5 * D ** -0.5), 0.4375, ((0, 16), (1, 32))),
        "token_mask": plant((jax.random.randint(keys[17], (ROWS, VOCAB), 0, 10) < 9).astype(jnp.int32), jax.random.fold_in(keys[17], 1), 0, 1),
        "min_share": plant(jax.random.randint(keys[18], (ROWS,), 1311, 13108), jax.random.fold_in(keys[18], 1), 1311, 13107).astype(jnp.int32),
    }


EPSILON = 1e-05
INVERSE_HEAT = 1.25
FIXED_POINT = 65536.0
NEG_LARGE = -1e+30

def conv_step(history, newest, filter_coefficient):
    window = jnp.concatenate([history, newest[:, None, :]], axis=1)
    mixed_taps = lax.optimization_barrier(jnp.sum(window.astype(jnp.float32) * filter_coefficient.astype(jnp.float32)[None, :, :], axis=1))
    return (window[:, 1:, :], jax.nn.silu(mixed_taps))

def leading(values_in):
    return jnp.moveaxis(values_in, 1, 0)

def one_group(items):
    state_old, inner_part, pair_part, steps, decays = items
    state_new = decays[:, :, None, None] * state_old.astype(jnp.float32) + (steps[:, :, None] * inner_part)[:, :, :, None] * pair_part[:, None, None, 0, :]
    readout = lax.optimization_barrier(jnp.sum(state_new * pair_part[:, None, None, 1, :], axis=3))
    return (state_new.astype(jnp.bfloat16), readout)

def reference(hidden, norm_gain, input_weight, group_weight, step_weight, conv_inner_weight, conv_group_weight, conv_inner_state, conv_group_state, timestep_bias, decay_log, skip_gain, recurrent_state, mixer_gain, output_weight, final_gain, lexicon_matrix, token_mask, min_share):
    hidden_wide = hidden.astype(jnp.float32)
    hidden_scale = lax.rsqrt(lax.optimization_barrier(jnp.mean(hidden_wide * hidden_wide, axis=1, keepdims=True)) + EPSILON)
    normed = (hidden_wide * hidden_scale * norm_gain.astype(jnp.float32)[None, :]).astype(jnp.bfloat16)
    gate_raw = jnp.dot(normed, input_weight[:, 0, :], preferred_element_type=jnp.float32)
    inner_raw = jnp.dot(normed, input_weight[:, 1, :], preferred_element_type=jnp.float32)
    group_raw = jnp.dot(normed, group_weight, preferred_element_type=jnp.float32)
    step_raw = jnp.dot(normed, step_weight, preferred_element_type=jnp.float32)
    next_conv_inner, conv_inner = conv_step(conv_inner_state, inner_raw.astype(jnp.bfloat16), conv_inner_weight)
    next_conv_group, conv_group = conv_step(conv_group_state, group_raw.astype(jnp.bfloat16), conv_group_weight)
    group_round = lax.optimization_barrier(conv_group.astype(jnp.bfloat16)).astype(jnp.float32)
    step_size = jax.nn.softplus(step_raw + timestep_bias[None, :])
    decay_rate = jnp.exp(-step_size * jnp.exp(decay_log)[None, :])
    heads_group = HEADS // GROUPS
    pair_groups = jnp.transpose(group_round.reshape(ROWS, 2, STATE, GROUPS), (0, 3, 1, 2))
    inner_groups = conv_inner.reshape(ROWS, GROUPS, heads_group, HEAD_DIM)
    state_groups = recurrent_state.reshape(ROWS, GROUPS, heads_group, HEAD_DIM, STATE)
    step_groups = step_size.reshape(ROWS, GROUPS, heads_group)
    decay_groups = decay_rate.reshape(ROWS, GROUPS, heads_group)
    states_new, readout = lax.map(one_group, (leading(state_groups), leading(inner_groups), leading(pair_groups), leading(step_groups), leading(decay_groups)))
    next_state = jnp.moveaxis(states_new, 0, 1).reshape(ROWS, HEADS, HEAD_DIM, STATE)
    readout = jnp.moveaxis(readout, 0, 1).reshape(ROWS, HEADS, HEAD_DIM)
    readout = readout + skip_gain[None, :, None] * conv_inner.reshape(ROWS, HEADS, HEAD_DIM)
    gated_out = readout.reshape(ROWS, HEADS * HEAD_DIM) * jax.nn.silu(gate_raw)
    gated_groups = gated_out.reshape(ROWS, GROUPS, HEADS * HEAD_DIM // GROUPS)
    group_total = lax.optimization_barrier(jnp.sum(gated_groups * gated_groups, axis=2, keepdims=True))
    group_scale = lax.rsqrt(group_total / (HEADS * HEAD_DIM // GROUPS) + EPSILON)
    mixer_in = ((gated_groups * group_scale).reshape(ROWS, HEADS * HEAD_DIM) * mixer_gain.astype(jnp.float32)[None, :]).astype(jnp.bfloat16)
    mixed = jnp.dot(mixer_in, output_weight, preferred_element_type=jnp.float32)
    layer_out = (hidden_wide + mixed).astype(jnp.bfloat16)
    out_wide = layer_out.astype(jnp.float32)
    out_scale = lax.rsqrt(lax.optimization_barrier(jnp.mean(out_wide * out_wide, axis=1, keepdims=True)) + EPSILON)
    last_rescaled_vector = (out_wide * out_scale * final_gain.astype(jnp.float32)[None, :]).astype(jnp.bfloat16)
    candidate_scores = jnp.dot(last_rescaled_vector, lexicon_matrix, preferred_element_type=jnp.float32) * INVERSE_HEAT
    allowed = token_mask > 0
    peak_logit = lax.optimization_barrier(jnp.max(jnp.where(allowed, candidate_scores, NEG_LARGE), axis=1, keepdims=True))
    ratio_to_peak = jnp.where(allowed, jnp.exp(candidate_scores - peak_logit), 0.0)
    floor_share = min_share.astype(jnp.float32)[:, None] / FIXED_POINT
    weights = ratio_to_peak * jnp.clip(ratio_to_peak / floor_share - 1.0, 0.0, 1.0)
    kept_total = lax.optimization_barrier(jnp.sum(weights, axis=1, keepdims=True))
    next_probs = (weights / kept_total).astype(jnp.bfloat16)
    return (next_state, next_conv_inner, next_conv_group, layer_out, next_probs)
```

```python
import jax
import jax.numpy as jnp
from jax import lax
from jax.experimental import pallas as pl
from jax.experimental.pallas import tpu as pltpu
from jax.sharding import PartitionSpec as P

D = 8192
HEADS = 256
HEAD_DIM = 64
STATE = 256
GROUPS = 8
NR = 16
NH = 32
ROWS = 32
EPSILON = 1e-05
INVERSE_HEAT = 1.25
FIXED_POINT = 65536.0
NEG_LARGE = -1e30
MESH = pl.DeviceIdType.MESH
BF = jnp.bfloat16
F32 = jnp.float32


def silu(v):
    return v / (1.0 + jnp.exp(-v))


def iota(shape, axis):
    return lax.broadcasted_iota(jnp.int32, shape, axis)


def dot(a, b):
    return jnp.dot(a, b, preferred_element_type=F32)


def dot_nt(a, b):
    return lax.dot_general(a, b, (((1,), (1,)), ((), ())), preferred_element_type=F32)


N_IN = 19
SMALL = (
    "hidden",
    "norm_gain",
    "group_weight",
    "step_weight",
    "conv_inner_weight",
    "conv_group_weight",
    "conv_inner_state",
    "conv_group_state",
    "mixer_gain",
    "final_gain",
    "token_mask",
    "recurrent_state",
    "output_weight",
    "lexicon_matrix",
    "timestep_bias",
    "decay_log",
    "skip_gain",
    "min_share",
)


def kernel(
    hidden_h,
    norm_gain_h,
    input_weight_h,
    group_weight_h,
    step_weight_h,
    conv_inner_weight_h,
    conv_group_weight_h,
    conv_inner_state_h,
    conv_group_state_h,
    timestep_bias_h,
    decay_log_h,
    skip_gain_h,
    recurrent_state_h,
    mixer_gain_h,
    output_weight_h,
    final_gain_h,
    lexicon_h,
    token_mask_h,
    min_share_h,
    next_state_h,
    next_conv_inner_h,
    next_conv_group_h,
    layer_out_h,
    next_probs_h,
    hidden_v,
    norm_gain_v,
    input_weight_v,
    group_weight_v,
    step_weight_v,
    conv_inner_weight_v,
    conv_group_weight_v,
    conv_inner_state_v,
    conv_group_state_v,
    recurrent_state_v,
    mixer_gain_v,
    output_weight_v,
    final_gain_v,
    lexicon_v,
    token_mask_v,
    next_state_v,
    next_conv_inner,
    next_conv_group,
    layer_out,
    next_probs,
    timestep_bias,
    decay_log,
    skip_gain,
    min_share,
    hidden_rows,
    square_buf,
    in_part,
    in_buf,
    pair_buf,
    share_buf,
    mixer_buf,
    mixed_part,
    mixed_buf,
    scale_buf,
    out_buf,
    logit_part,
    logit_buf,
    peak_buf,
    total_buf,
    in_sem,
    weight_sem,
    save_sem,
    send_sem,
    recv_sem,
):
    i = lax.axis_index("row")
    j = lax.axis_index("head")

    loads = {
        "hidden": (hidden_h, hidden_v),
        "norm_gain": (norm_gain_h, norm_gain_v),
        "group_weight": (group_weight_h, group_weight_v),
        "step_weight": (step_weight_h, step_weight_v),
        "conv_inner_weight": (conv_inner_weight_h, conv_inner_weight_v),
        "conv_group_weight": (conv_group_weight_h, conv_group_weight_v),
        "conv_inner_state": (conv_inner_state_h, conv_inner_state_v),
        "conv_group_state": (conv_group_state_h, conv_group_state_v),
        "mixer_gain": (mixer_gain_h, mixer_gain_v),
        "final_gain": (final_gain_h, final_gain_v),
        "token_mask": (token_mask_h, token_mask_v),
        "recurrent_state": (recurrent_state_h, recurrent_state_v),
        "output_weight": (output_weight_h, output_weight_v),
        "lexicon_matrix": (lexicon_h, lexicon_v),
        "timestep_bias": (timestep_bias_h, timestep_bias),
        "decay_log": (decay_log_h, decay_log),
        "skip_gain": (skip_gain_h, skip_gain),
        "min_share": (min_share_h, min_share),
    }

    def load(name):
        src, dst = loads[name]
        return pltpu.make_async_copy(src, dst, in_sem.at[SMALL.index(name)])

    def load_weight(block):
        return pltpu.make_async_copy(
            input_weight_h.at[:, :, pl.ds(block * 128, 128)],
            input_weight_v.at[block],
            weight_sem.at[block],
        )

    load("hidden").start()
    load("norm_gain").start()
    for block in range(4):
        load_weight(block).start()
    for name in SMALL[2:]:
        load(name).start()

    barrier = pltpu.get_barrier_semaphore()

    def greet_row(k, carry):
        pl.semaphore_signal(barrier, inc=1, device_id=(lax.rem(i + k, NR), j), device_id_type=MESH)
        return carry

    def greet_head(k, carry):
        pl.semaphore_signal(barrier, inc=1, device_id=(i, lax.rem(j + k, NH)), device_id_type=MESH)
        return carry

    lax.fori_loop(1, NR, greet_row, 0)
    lax.fori_loop(1, NH, greet_head, 0)

    def send_row(phase, src, dst):
        def step(k, carry):
            to = lax.rem(i + k, NR)
            pltpu.make_async_remote_copy(
                src_ref=dst.at[i] if src is None else src.at[to],
                dst_ref=dst.at[i],
                send_sem=send_sem.at[phase],
                recv_sem=recv_sem.at[phase],
                device_id=(to, j),
                device_id_type=MESH,
            ).start()
            return carry

        lax.fori_loop(1, NR, step, 0)

    def send_head(phase, src, dst):
        def step(k, carry):
            to = lax.rem(j + k, NH)
            pltpu.make_async_remote_copy(
                src_ref=dst.at[j] if src is None else src.at[to],
                dst_ref=dst.at[j],
                send_sem=send_sem.at[phase],
                recv_sem=recv_sem.at[phase],
                device_id=(i, to),
                device_id_type=MESH,
            ).start()
            return carry

        lax.fori_loop(1, NH, step, 0)

    def arrived(phase, dst):
        rest = dst.at[pl.ds(0, dst.shape[0] - 1)]
        pltpu.make_async_copy(rest, rest, recv_sem.at[phase]).wait()

    def sent(phase, dst):
        rest = dst.at[pl.ds(0, dst.shape[0] - 1)]
        pltpu.make_async_copy(rest, rest, send_sem.at[phase]).wait()

    def send_group(phase, dst):
        first = j - j % 4

        def step(k, carry):
            to = first + lax.rem(j + k, 4)
            pltpu.make_async_remote_copy(
                src_ref=dst.at[j % 4],
                dst_ref=dst.at[j % 4],
                send_sem=send_sem.at[phase],
                recv_sem=recv_sem.at[phase],
                device_id=(i, to),
                device_id_type=MESH,
            ).start()
            return carry

        lax.fori_loop(1, 4, step, 0)

    def save(at, src, dst):
        copy = pltpu.make_async_copy(src, dst, save_sem.at[at])
        copy.start()
        return copy

    load("hidden").wait()
    load("norm_gain").wait()
    hidden_wide = hidden_v[...].astype(F32)
    hidden_rows[:, 0, :] = hidden_wide
    squares = jnp.sum(hidden_wide * hidden_wide, axis=1, keepdims=True)
    diagonal = iota((ROWS, 128), 0) == iota((ROWS, 128), 1)
    square_buf[i] = jnp.sum(jnp.where(diagonal, squares, 0.0), axis=0, keepdims=True)
    pl.semaphore_wait(barrier, NR + NH - 2)
    send_row(8, None, square_buf)
    arrived(8, square_buf)
    square_total = jnp.sum(square_buf[:, 0, :], axis=0, keepdims=True)
    row_total = jnp.sum(jnp.where(diagonal, square_total, 0.0), axis=1, keepdims=True)
    hidden_scale = lax.rsqrt(row_total / D + EPSILON)

    gained = (hidden_wide * hidden_scale * norm_gain_v[...].astype(F32).reshape(1, 512)).astype(BF)
    depth_at, slot_at = iota((128, 256), 0), iota((128, 256), 1)
    spread_even = (slot_at == 2 * depth_at).astype(F32).astype(BF)
    spread_odd = (slot_at == 2 * depth_at + 1).astype(F32).astype(BF)
    blocks = [gained[:, 128 * b : 128 * b + 128] for b in range(4)]
    doubled = jnp.concatenate(
        [
            jnp.concatenate([dot(part, spread_even) for part in blocks], axis=1),
            jnp.concatenate([dot(part, spread_odd) for part in blocks], axis=1),
        ],
        axis=0,
    ).astype(BF)
    for block in range(4):
        load_weight(block).wait()
        both = dot(doubled, input_weight_v[block].reshape(1024, 128))
        in_part[:, :, 128 * block : 128 * block + 128] = both[:32].reshape(NR, 2, 128)
        in_part[:, :, 512 + 128 * block : 640 + 128 * block] = both[32:].reshape(NR, 2, 128)
    load("group_weight").wait()
    in_part[:, :, 1024:1152] = dot(gained, group_weight_v[...]).reshape(NR, 2, 128)
    load("step_weight").wait()
    step_rows = jnp.concatenate(
        [step_weight_v[...].astype(F32), jnp.zeros((120, 512), F32)], axis=0
    ).astype(BF)
    in_part[:, :, 1152:1280] = dot_nt(gained, step_rows).reshape(NR, 2, 128)
    send_row(0, in_part, in_buf)
    in_buf[i] = in_part[i]

    for name in ("conv_inner_weight", "conv_group_weight", "conv_inner_state", "conv_group_state"):
        load(name).wait()
    arrived(0, in_buf)
    projected = jnp.sum(in_buf[...], axis=0)
    group_new = (projected[:, 1024:1152]).astype(BF)
    group_old = conv_group_state_v[...].astype(F32)
    group_taps = conv_group_weight_v[...].astype(F32)
    group_mix = (
        group_old[0] * group_taps[0:1]
        + group_old[1] * group_taps[1:2]
        + group_old[2] * group_taps[2:3]
        + group_new.astype(F32) * group_taps[3:4]
    )
    pair_buf[j] = silu(group_mix).astype(BF).astype(F32)
    send_head(1, None, pair_buf)

    next_conv_group[0] = conv_group_state_v[1]
    next_conv_group[1] = conv_group_state_v[2]
    next_conv_group[2] = group_new
    inner_new = (projected[:, 512:1024]).astype(BF)
    next_conv_inner[0] = conv_inner_state_v[1]
    next_conv_inner[1] = conv_inner_state_v[2]
    next_conv_inner[2] = inner_new
    inner_old = conv_inner_state_v[...].astype(F32)
    inner_taps = conv_inner_weight_v[...].astype(F32)
    conv_inner = silu(
        inner_old[0] * inner_taps[0:1]
        + inner_old[1] * inner_taps[1:2]
        + inner_old[2] * inner_taps[2:3]
        + inner_new.astype(F32) * inner_taps[3:4]
    )
    gate = silu(projected[:, :512])
    step_raw = projected[:, 1152:1160]
    saves = [
        save(1, next_conv_inner, next_conv_inner_h),
        save(2, next_conv_group, next_conv_group_h),
    ]
    for name in ("timestep_bias", "decay_log", "skip_gain"):
        load(name).wait()
    head_of = iota((2, 512), 1) // HEAD_DIM
    step_in = jnp.zeros((2, 512), F32)
    rate_log = jnp.zeros((2, 512), F32)
    skip = jnp.zeros((2, 512), F32)
    for h in range(8):
        here = head_of == h
        step_in = jnp.where(here, step_raw[:, h : h + 1] + timestep_bias[h], step_in)
        rate_log = jnp.where(here, decay_log[h], rate_log)
        skip = jnp.where(here, skip_gain[h], skip)
    step_size = jnp.maximum(step_in, 0.0) + jnp.log1p(jnp.exp(-jnp.abs(step_in)))
    decay = jnp.exp(-step_size * jnp.exp(rate_log))
    driven = step_size * conv_inner

    group_at = j // (NH // GROUPS)
    channel_at, entry_at = iota((128, 256), 0), iota((128, 256), 1)
    pick = (channel_at == (entry_at % 16) * GROUPS + group_at).astype(F32).astype(BF)
    source_at, entry_of = iota((NH, 256), 0), iota((NH, 256), 1) // 16
    load("recurrent_state").wait()
    load("mixer_gain").wait()
    arrived(1, pair_buf)
    inputs, readouts = [], []
    for r in range(2):
        picked = dot(pair_buf[:, r, :].astype(BF), pick)
        inputs.append(
            jnp.sum(jnp.where(source_at == entry_of, picked, 0.0), axis=0, keepdims=True)
        )
        readouts.append(
            jnp.sum(jnp.where(source_at == entry_of + 16, picked, 0.0), axis=0, keepdims=True)
        )
    readout = []
    for r in range(2):
        old_read = dot_nt(readouts[r].astype(BF), recurrent_state_v[r].reshape(512, 256))
        pair_dot = jnp.sum(inputs[r] * readouts[r], axis=1, keepdims=True)
        readout.append(
            decay[r : r + 1] * old_read
            + driven[r : r + 1] * pair_dot
            + skip[r : r + 1] * conv_inner[r : r + 1]
        )
    gated = jnp.concatenate(readout, axis=0) * gate
    gated_squares = jnp.sum(gated * gated, axis=1, keepdims=True)
    mixer_gain_wide = mixer_gain_v[...].astype(F32).reshape(1, 512)
    share_buf[j % 4] = jnp.broadcast_to(gated_squares, (2, 128))
    send_group(9, share_buf)
    arrived(9, share_buf)
    group_total = jnp.sum(share_buf[...], axis=0)[:, 0:1]
    group_scale = lax.rsqrt(group_total / (HEADS * HEAD_DIM // GROUPS) + EPSILON)
    mixer_buf[i] = (gated * group_scale * mixer_gain_wide).astype(BF).astype(F32)
    send_row(2, None, mixer_buf)

    rows8 = jnp.concatenate([driven, decay, jnp.zeros((4, 512), F32)], axis=0)
    columns = rows8.T
    for r in range(2):
        for h in range(8):
            at = slice(64 * h, 64 * h + 64)
            fresh = (
                columns[at, 2 + r : 3 + r] * recurrent_state_v[r, h].astype(F32)
                + columns[at, r : r + 1] * inputs[r]
            )
            next_state_v[r, h] = fresh.astype(BF)
    saves.append(save(0, next_state_v, next_state_h))

    load("output_weight").wait()
    arrived(2, mixer_buf)
    mixer_rows = mixer_buf[...].reshape(ROWS, 512).astype(BF)
    mixed_part[:, 0, :] = dot(mixer_rows, output_weight_v[...])
    send_head(3, mixed_part, mixed_buf)
    mixed_buf[j] = mixed_part[j]

    arrived(3, mixed_buf)
    mixed = jnp.sum(mixed_buf[:, 0, :], axis=0, keepdims=True)
    out_mine = (hidden_rows[j] + mixed).astype(BF).astype(F32)
    scale_buf[i] = jnp.broadcast_to(jnp.sum(out_mine * out_mine, axis=1, keepdims=True), (1, 128))
    send_row(10, None, scale_buf)
    arrived(10, scale_buf)
    out_buf[j, :, 0:512] = out_mine
    out_buf[j, :, 512:640] = jnp.sum(scale_buf[:, 0, :], axis=0, keepdims=True)
    send_head(4, None, out_buf)

    load("final_gain").wait()
    load("lexicon_matrix").wait()
    load("token_mask").wait()
    load("min_share").wait()
    final_gain_wide = final_gain_v[...].astype(F32).reshape(1, 512)
    arrived(4, out_buf)
    out_wide = out_buf[:, 0, 0:512]
    out_scale = lax.rsqrt(out_buf[:, 0, 512:640][:, 0:1] / D + EPSILON)
    final_rows = (out_wide * out_scale * final_gain_wide).astype(BF)
    for block in range(4):
        at = slice(512 * block, 512 * block + 512)
        logit_part[:, :, at] = dot(final_rows, lexicon_v[:, at]).reshape(NR, 2, 512)
    send_row(5, logit_part, logit_buf)
    logit_buf[i] = logit_part[i]
    layer_out[...] = out_wide.astype(BF)
    saves.append(save(3, layer_out, layer_out_h))

    allowed = token_mask_v[...] > 0
    row_at = iota((2, 1), 0)
    floor_share = (
        jnp.where(row_at == 0, min_share[0], min_share[1]).astype(F32) / FIXED_POINT
    )
    arrived(5, logit_buf)
    scores = jnp.sum(logit_buf[...], axis=0) * INVERSE_HEAT
    peak_mine = jnp.max(jnp.where(allowed, scores, NEG_LARGE), axis=1, keepdims=True)
    peak_buf[j] = jnp.broadcast_to(peak_mine, (2, 128))
    send_head(6, None, peak_buf)
    arrived(6, peak_buf)
    peak = jnp.max(peak_buf[...], axis=0)[:, 0:1]
    ratio = jnp.where(allowed, jnp.exp(scores - peak), 0.0)
    weights = ratio * jnp.clip(ratio / floor_share - 1.0, 0.0, 1.0)
    total_mine = jnp.sum(weights, axis=1, keepdims=True)
    total_buf[j] = jnp.broadcast_to(total_mine, (2, 128))
    send_head(7, None, total_buf)
    arrived(7, total_buf)
    total = jnp.sum(total_buf[...], axis=0)[:, 0:1]
    next_probs[...] = (weights / total).astype(BF)

    saves.append(save(4, next_probs, next_probs_h))
    for copy in saves:
        copy.wait()
    for phase, dst in enumerate(
        (
            in_buf,
            pair_buf,
            mixer_buf,
            mixed_buf,
            out_buf,
            logit_buf,
            peak_buf,
            total_buf,
            square_buf,
            share_buf,
            scale_buf,
        )
    ):
        sent(phase, dst)


def local(
    hidden,
    norm_gain,
    input_weight,
    group_weight,
    step_weight,
    conv_inner_weight,
    conv_group_weight,
    conv_inner_state,
    conv_group_state,
    timestep_bias,
    decay_log,
    skip_gain,
    recurrent_state,
    mixer_gain,
    output_weight,
    final_gain,
    lexicon_matrix,
    token_mask,
    min_share,
):
    hbm = pl.BlockSpec(memory_space=pltpu.HBM)
    in_specs = [hbm] * N_IN
    state, inner, group, out, probs = pl.pallas_call(
        kernel,
        out_shape=(
            jax.ShapeDtypeStruct((2, 8, 64, 256), BF),
            jax.ShapeDtypeStruct((3, 2, 512), BF),
            jax.ShapeDtypeStruct((3, 2, 128), BF),
            jax.ShapeDtypeStruct((ROWS, 512), BF),
            jax.ShapeDtypeStruct((2, 2048), BF),
        ),
        in_specs=in_specs,
        out_specs=(hbm,) * 5,
        scratch_shapes=[
            pltpu.VMEM((ROWS, 512), BF),
            pltpu.VMEM((512,), BF),
            pltpu.VMEM((4, 512, 2, 128), BF),
            pltpu.VMEM((512, 128), BF),
            pltpu.VMEM((8, 512), BF),
            pltpu.VMEM((4, 512), BF),
            pltpu.VMEM((4, 128), BF),
            pltpu.VMEM((3, 2, 512), BF),
            pltpu.VMEM((3, 2, 128), BF),
            pltpu.VMEM((2, 8, 64, 256), BF),
            pltpu.VMEM((512,), BF),
            pltpu.VMEM((512, 512), BF),
            pltpu.VMEM((512,), BF),
            pltpu.VMEM((512, 2048), BF),
            pltpu.VMEM((2, 2048), jnp.int32),
            pltpu.VMEM((2, 8, 64, 256), BF),
            pltpu.VMEM((3, 2, 512), BF),
            pltpu.VMEM((3, 2, 128), BF),
            pltpu.VMEM((ROWS, 512), BF),
            pltpu.VMEM((2, 2048), BF),
            pltpu.SMEM((8,), F32),
            pltpu.SMEM((8,), F32),
            pltpu.SMEM((8,), F32),
            pltpu.SMEM((2,), jnp.int32),
            pltpu.VMEM((ROWS, 1, 512), F32),
            pltpu.VMEM((NR, 1, 128), F32),
            pltpu.VMEM((NR, 2, 1280), F32),
            pltpu.VMEM((NR, 2, 1280), F32),
            pltpu.VMEM((NH, 2, 128), F32),
            pltpu.VMEM((4, 2, 128), F32),
            pltpu.VMEM((NR, 2, 512), F32),
            pltpu.VMEM((ROWS, 1, 512), F32),
            pltpu.VMEM((NH, 1, 512), F32),
            pltpu.VMEM((NR, 1, 128), F32),
            pltpu.VMEM((NH, 1, 640), F32),
            pltpu.VMEM((NR, 2, 2048), F32),
            pltpu.VMEM((NR, 2, 2048), F32),
            pltpu.VMEM((NH, 2, 128), F32),
            pltpu.VMEM((NH, 2, 128), F32),
            pltpu.SemaphoreType.DMA((len(SMALL),)),
            pltpu.SemaphoreType.DMA((4,)),
            pltpu.SemaphoreType.DMA((5,)),
            pltpu.SemaphoreType.DMA((11,)),
            pltpu.SemaphoreType.DMA((11,)),
        ],
        compiler_params=pltpu.CompilerParams(
            collective_id=0, has_side_effects=True, vmem_limit_bytes=56 << 20
        ),
    )(
        hidden,
        norm_gain,
        input_weight,
        group_weight,
        step_weight.T,
        conv_inner_weight,
        conv_group_weight,
        jnp.transpose(conv_inner_state, (1, 0, 2)),
        jnp.transpose(conv_group_state, (1, 0, 2)),
        timestep_bias,
        decay_log,
        skip_gain,
        recurrent_state,
        mixer_gain,
        output_weight,
        final_gain,
        lexicon_matrix,
        token_mask,
        min_share,
    )
    return (
        state,
        jnp.transpose(inner, (1, 0, 2)),
        jnp.transpose(group, (1, 0, 2)),
        out,
        probs,
    )


def solution(mesh):
    in_specs = (
        P(None, "row"),
        P("row"),
        P("row", None, "head"),
        P("row", "head"),
        P("row", "head"),
        P(None, "head"),
        P(None, "head"),
        P("row", None, "head"),
        P("row", None, "head"),
        P("head"),
        P("head"),
        P("head"),
        P("row", "head", None, None),
        P("head"),
        P("head", "row"),
        P("row"),
        P("row", "head"),
        P("row", "head"),
        P("row"),
    )
    out_specs = (
        P("row", "head", None, None),
        P("row", None, "head"),
        P("row", None, "head"),
        P(None, "row"),
        P("row", "head"),
    )
    return jax.shard_map(local, mesh=mesh, in_specs=in_specs, out_specs=out_specs, check_vma=False)
```

```python
import jax
import jax.numpy as jnp
from jax import lax
from jax.experimental import pallas as pl
from jax.experimental.pallas import tpu as pltpu
from jax.sharding import PartitionSpec as P

D = 8192
HEADS = 256
HEAD_DIM = 64
STATE = 256
GROUPS = 8
NR = 16
NH = 32
ROWS = 32
EPSILON = 1e-05
INVERSE_HEAT = 1.25
FIXED_POINT = 65536.0
NEG_LARGE = -1e30
MESH = pl.DeviceIdType.MESH
BF = jnp.bfloat16
F32 = jnp.float32


def silu(v):
    return v / (1.0 + jnp.exp(-v))


def iota(shape, axis):
    return lax.broadcasted_iota(jnp.int32, shape, axis)


def dot(a, b):
    return jnp.dot(a, b, preferred_element_type=F32)


def dot_nt(a, b):
    return lax.dot_general(a, b, (((1,), (1,)), ((), ())), preferred_element_type=F32)


N_IN = 19
SMALL = (
    "hidden",
    "norm_gain",
    "group_weight",
    "step_weight",
    "conv_inner_weight",
    "conv_group_weight",
    "conv_inner_state",
    "conv_group_state",
    "mixer_gain",
    "final_gain",
    "token_mask",
    "recurrent_state",
    "output_weight",
    "lexicon_matrix",
    "timestep_bias",
    "decay_log",
    "skip_gain",
    "min_share",
)


def kernel(
    hidden_h,
    norm_gain_h,
    input_weight_h,
    group_weight_h,
    step_weight_h,
    conv_inner_weight_h,
    conv_group_weight_h,
    conv_inner_state_h,
    conv_group_state_h,
    timestep_bias_h,
    decay_log_h,
    skip_gain_h,
    recurrent_state_h,
    mixer_gain_h,
    output_weight_h,
    final_gain_h,
    lexicon_h,
    token_mask_h,
    min_share_h,
    next_state_h,
    next_conv_inner_h,
    next_conv_group_h,
    layer_out_h,
    next_probs_h,
    hidden_v,
    norm_gain_v,
    input_weight_v,
    group_weight_v,
    step_weight_v,
    conv_inner_weight_v,
    conv_group_weight_v,
    conv_inner_state_v,
    conv_group_state_v,
    recurrent_state_v,
    mixer_gain_v,
    output_weight_v,
    final_gain_v,
    lexicon_v,
    token_mask_v,
    next_state_v,
    next_conv_inner,
    next_conv_group,
    layer_out,
    next_probs,
    timestep_bias,
    decay_log,
    skip_gain,
    min_share,
    hidden_rows,
    square_buf,
    group_part,
    group_buf,
    in_part,
    in_buf,
    pair_buf,
    share_buf,
    mixer_buf,
    mixed_part,
    mixed_buf,
    scale_buf,
    out_buf,
    logit_part,
    logit_buf,
    peak_buf,
    total_buf,
    in_sem,
    weight_sem,
    save_sem,
    send_sem,
    recv_sem,
):
    i = lax.axis_index("row")
    j = lax.axis_index("head")

    loads = {
        "hidden": (hidden_h, hidden_v),
        "norm_gain": (norm_gain_h, norm_gain_v),
        "group_weight": (group_weight_h, group_weight_v),
        "step_weight": (step_weight_h, step_weight_v),
        "conv_inner_weight": (conv_inner_weight_h, conv_inner_weight_v),
        "conv_group_weight": (conv_group_weight_h, conv_group_weight_v),
        "conv_inner_state": (conv_inner_state_h, conv_inner_state_v),
        "conv_group_state": (conv_group_state_h, conv_group_state_v),
        "mixer_gain": (mixer_gain_h, mixer_gain_v),
        "final_gain": (final_gain_h, final_gain_v),
        "token_mask": (token_mask_h, token_mask_v),
        "recurrent_state": (recurrent_state_h, recurrent_state_v),
        "output_weight": (output_weight_h, output_weight_v),
        "lexicon_matrix": (lexicon_h, lexicon_v),
        "timestep_bias": (timestep_bias_h, timestep_bias),
        "decay_log": (decay_log_h, decay_log),
        "skip_gain": (skip_gain_h, skip_gain),
        "min_share": (min_share_h, min_share),
    }

    def load(name):
        src, dst = loads[name]
        return pltpu.make_async_copy(src, dst, in_sem.at[SMALL.index(name)])

    def load_weight(block):
        return pltpu.make_async_copy(
            input_weight_h.at[:, :, pl.ds(block * 128, 128)],
            input_weight_v.at[block],
            weight_sem.at[block],
        )

    load("hidden").start()
    load("norm_gain").start()
    for block in range(4):
        load_weight(block).start()
    for name in SMALL[2:]:
        load(name).start()

    barrier = pltpu.get_barrier_semaphore()

    def far_first(k, n):
        return n // 2 + (2 * (k % 2) - 1) * ((k + 1) // 2)

    def greet_row(k, carry):
        to = lax.rem(i + far_first(k, NR), NR)
        pl.semaphore_signal(barrier, inc=1, device_id=(to, j), device_id_type=MESH)
        return carry

    def greet_head(k, carry):
        to = lax.rem(j + far_first(k, NH), NH)
        pl.semaphore_signal(barrier, inc=1, device_id=(i, to), device_id_type=MESH)
        return carry

    lax.fori_loop(0, NR - 1, greet_row, 0)
    lax.fori_loop(0, NH - 1, greet_head, 0)

    def send_row(phase, src, dst):
        def step(k, carry):
            to = lax.rem(i + far_first(k, NR), NR)
            pltpu.make_async_remote_copy(
                src_ref=dst.at[i] if src is None else src.at[to],
                dst_ref=dst.at[i],
                send_sem=send_sem.at[phase],
                recv_sem=recv_sem.at[phase],
                device_id=(to, j),
                device_id_type=MESH,
            ).start()
            return carry

        lax.fori_loop(0, NR - 1, step, 0)

    def send_head(phase, src, dst):
        def step(k, carry):
            to = lax.rem(j + far_first(k, NH), NH)
            pltpu.make_async_remote_copy(
                src_ref=dst.at[j] if src is None else src.at[to],
                dst_ref=dst.at[j],
                send_sem=send_sem.at[phase],
                recv_sem=recv_sem.at[phase],
                device_id=(i, to),
                device_id_type=MESH,
            ).start()
            return carry

        lax.fori_loop(0, NH - 1, step, 0)

    def arrived(phase, dst):
        rest = dst.at[pl.ds(0, dst.shape[0] - 1)]
        pltpu.make_async_copy(rest, rest, recv_sem.at[phase]).wait()

    def sent(phase, dst):
        rest = dst.at[pl.ds(0, dst.shape[0] - 1)]
        pltpu.make_async_copy(rest, rest, send_sem.at[phase]).wait()

    def send_group(phase, dst):
        first = j - j % 4

        def step(k, carry):
            to = first + lax.rem(j + k, 4)
            pltpu.make_async_remote_copy(
                src_ref=dst.at[j % 4],
                dst_ref=dst.at[j % 4],
                send_sem=send_sem.at[phase],
                recv_sem=recv_sem.at[phase],
                device_id=(i, to),
                device_id_type=MESH,
            ).start()
            return carry

        lax.fori_loop(1, 4, step, 0)

    def save(at, src, dst):
        copy = pltpu.make_async_copy(src, dst, save_sem.at[at])
        copy.start()
        return copy

    load("hidden").wait()
    load("norm_gain").wait()
    hidden_wide = hidden_v[...].astype(F32)
    hidden_rows[:, 0, :] = hidden_wide
    squares = jnp.sum(hidden_wide * hidden_wide, axis=1, keepdims=True)
    diagonal = iota((ROWS, 128), 0) == iota((ROWS, 128), 1)
    square_buf[i] = jnp.sum(jnp.where(diagonal, squares, 0.0), axis=0, keepdims=True)
    depth_at, slot_at = iota((128, 256), 0), iota((128, 256), 1)
    spread_even = (slot_at == 2 * depth_at).astype(F32).astype(BF)
    spread_odd = (slot_at == 2 * depth_at + 1).astype(F32).astype(BF)
    load("group_weight").wait()
    pl.semaphore_wait(barrier, NR + NH - 2)
    send_row(8, None, square_buf)
    arrived(8, square_buf)
    square_total = jnp.sum(square_buf[:, 0, :], axis=0, keepdims=True)
    row_total = jnp.sum(jnp.where(diagonal, square_total, 0.0), axis=1, keepdims=True)
    hidden_scale = lax.rsqrt(row_total / D + EPSILON)

    gained = (hidden_wide * hidden_scale * norm_gain_v[...].astype(F32).reshape(1, 512)).astype(BF)
    group_part[...] = dot(gained, group_weight_v[...]).reshape(NR, 2, 128)
    send_row(0, group_part, group_buf)
    group_buf[i] = group_part[i]
    blocks = [gained[:, 128 * b : 128 * b + 128] for b in range(4)]
    doubled = jnp.concatenate(
        [
            jnp.concatenate([dot(part, spread_even) for part in blocks], axis=1),
            jnp.concatenate([dot(part, spread_odd) for part in blocks], axis=1),
        ],
        axis=0,
    ).astype(BF)
    for block in range(4):
        load_weight(block).wait()
        both = dot(doubled, input_weight_v[block].reshape(1024, 128))
        in_part[:, :, 128 * block : 128 * block + 128] = both[:32].reshape(NR, 2, 128)
        in_part[:, :, 512 + 128 * block : 640 + 128 * block] = both[32:].reshape(NR, 2, 128)
    load("step_weight").wait()
    step_rows = jnp.concatenate(
        [step_weight_v[...].astype(F32), jnp.zeros((120, 512), F32)], axis=0
    ).astype(BF)
    in_part[:, :, 1024:1152] = dot_nt(gained, step_rows).reshape(NR, 2, 128)
    send_row(11, in_part, in_buf)
    in_buf[i] = in_part[i]

    for name in ("conv_inner_weight", "conv_group_weight", "conv_inner_state", "conv_group_state"):
        load(name).wait()
    arrived(0, group_buf)
    group_new = jnp.sum(group_buf[...], axis=0).astype(BF)
    group_old = conv_group_state_v[...].astype(F32)
    group_taps = conv_group_weight_v[...].astype(F32)
    group_mix = (
        group_old[0] * group_taps[0:1]
        + group_old[1] * group_taps[1:2]
        + group_old[2] * group_taps[2:3]
        + group_new.astype(F32) * group_taps[3:4]
    )
    pair_buf[j] = silu(group_mix).astype(BF)
    send_head(1, None, pair_buf)

    next_conv_group[0] = conv_group_state_v[1]
    next_conv_group[1] = conv_group_state_v[2]
    next_conv_group[2] = group_new
    arrived(11, in_buf)
    projected = jnp.sum(in_buf[...], axis=0)
    inner_new = projected[:, 512:1024].astype(BF)
    next_conv_inner[0] = conv_inner_state_v[1]
    next_conv_inner[1] = conv_inner_state_v[2]
    next_conv_inner[2] = inner_new
    inner_old = conv_inner_state_v[...].astype(F32)
    inner_taps = conv_inner_weight_v[...].astype(F32)
    conv_inner = silu(
        inner_old[0] * inner_taps[0:1]
        + inner_old[1] * inner_taps[1:2]
        + inner_old[2] * inner_taps[2:3]
        + inner_new.astype(F32) * inner_taps[3:4]
    )
    gate = silu(projected[:, :512])
    step_raw = projected[:, 1024:1032]
    saves = [
        save(1, next_conv_inner, next_conv_inner_h),
        save(2, next_conv_group, next_conv_group_h),
    ]
    for name in ("timestep_bias", "decay_log", "skip_gain"):
        load(name).wait()
    head_of = iota((2, 512), 1) // HEAD_DIM
    step_in = jnp.zeros((2, 512), F32)
    rate_log = jnp.zeros((2, 512), F32)
    skip = jnp.zeros((2, 512), F32)
    for h in range(8):
        here = head_of == h
        step_in = jnp.where(here, step_raw[:, h : h + 1] + timestep_bias[h], step_in)
        rate_log = jnp.where(here, decay_log[h], rate_log)
        skip = jnp.where(here, skip_gain[h], skip)
    step_size = jnp.maximum(step_in, 0.0) + jnp.log1p(jnp.exp(-jnp.abs(step_in)))
    decay = jnp.exp(-step_size * jnp.exp(rate_log))
    driven = step_size * conv_inner

    group_at = j // (NH // GROUPS)
    channel_at, entry_at = iota((128, 256), 0), iota((128, 256), 1)
    pick = (channel_at == (entry_at % 16) * GROUPS + group_at).astype(F32).astype(BF)
    source_at, entry_of = iota((NH, 256), 0), iota((NH, 256), 1) // 16
    load("recurrent_state").wait()
    load("mixer_gain").wait()
    arrived(1, pair_buf)
    inputs, readouts = [], []
    for r in range(2):
        picked = dot(pair_buf[:, r, :], pick)
        inputs.append(
            jnp.sum(jnp.where(source_at == entry_of, picked, 0.0), axis=0, keepdims=True)
        )
        readouts.append(
            jnp.sum(jnp.where(source_at == entry_of + 16, picked, 0.0), axis=0, keepdims=True)
        )
    readout = []
    for r in range(2):
        old_read = dot_nt(readouts[r].astype(BF), recurrent_state_v[r].reshape(512, 256))
        pair_dot = jnp.sum(inputs[r] * readouts[r], axis=1, keepdims=True)
        readout.append(
            decay[r : r + 1] * old_read
            + driven[r : r + 1] * pair_dot
            + skip[r : r + 1] * conv_inner[r : r + 1]
        )
    gated = jnp.concatenate(readout, axis=0) * gate
    gated_squares = jnp.sum(gated * gated, axis=1, keepdims=True)
    mixer_gain_wide = mixer_gain_v[...].astype(F32).reshape(1, 512)
    share_buf[j % 4] = jnp.broadcast_to(gated_squares, (2, 128))
    send_group(9, share_buf)
    arrived(9, share_buf)
    group_total = jnp.sum(share_buf[...], axis=0)[:, 0:1]
    group_scale = lax.rsqrt(group_total / (HEADS * HEAD_DIM // GROUPS) + EPSILON)
    mixer_buf[i] = (gated * group_scale * mixer_gain_wide).astype(BF)
    send_row(2, None, mixer_buf)

    rows8 = jnp.concatenate([driven, decay, jnp.zeros((4, 512), F32)], axis=0)
    columns = rows8.T
    for r in range(2):
        for h in range(8):
            at = slice(64 * h, 64 * h + 64)
            fresh = (
                columns[at, 2 + r : 3 + r] * recurrent_state_v[r, h].astype(F32)
                + columns[at, r : r + 1] * inputs[r]
            )
            next_state_v[r, h] = fresh.astype(BF)
    saves.append(save(0, next_state_v, next_state_h))

    load("output_weight").wait()
    arrived(2, mixer_buf)
    mixer_rows = mixer_buf[...].reshape(ROWS, 512)
    mixed_part[:, 0, :] = dot(mixer_rows, output_weight_v[...])
    send_head(3, mixed_part, mixed_buf)
    mixed_buf[j] = mixed_part[j]

    load("final_gain").wait()
    final_gain_wide = final_gain_v[...].astype(F32).reshape(1, 512)
    arrived(3, mixed_buf)
    mixed = jnp.sum(mixed_buf[:, 0, :], axis=0, keepdims=True)
    out_rounded = (hidden_rows[j] + mixed).astype(BF)
    out_mine = out_rounded.astype(F32)
    scale_buf[i] = jnp.broadcast_to(jnp.sum(out_mine * out_mine, axis=1, keepdims=True), (1, 128))
    send_row(10, None, scale_buf)
    arrived(10, scale_buf)
    out_total = jnp.sum(scale_buf[:, 0, :], axis=0, keepdims=True)[:, 0:1]
    out_scale = lax.rsqrt(out_total / D + EPSILON)
    final_mine = (out_mine * out_scale * final_gain_wide).astype(BF).astype(F32)
    out_buf[j] = jnp.concatenate([final_mine, out_mine], axis=0).astype(BF)
    send_head(4, None, out_buf)

    load("lexicon_matrix").wait()
    load("token_mask").wait()
    load("min_share").wait()
    arrived(4, out_buf)
    final_rows = out_buf[:, 0, :]
    for block in range(4):
        at = slice(512 * block, 512 * block + 512)
        logit_part[block] = dot(final_rows, lexicon_v[:, at]).reshape(NR, 2, 512)
        send_row(12 + block, logit_part.at[block], logit_buf.at[block])
        logit_buf[block, i] = logit_part[block, i]
    layer_out[...] = out_buf[:, 1, :]
    saves.append(save(3, layer_out, layer_out_h))

    allowed = token_mask_v[...] > 0
    row_at = iota((2, 1), 0)
    floor_share = (
        jnp.where(row_at == 0, min_share[0], min_share[1]).astype(F32) / FIXED_POINT
    )
    sums = []
    for block in range(4):
        arrived(12 + block, logit_buf.at[block])
        sums.append(jnp.sum(logit_buf[block], axis=0))
    scores = jnp.concatenate(sums, axis=1) * INVERSE_HEAT
    peak_mine = jnp.max(jnp.where(allowed, scores, NEG_LARGE), axis=1, keepdims=True)
    peak_buf[j] = jnp.broadcast_to(peak_mine, (2, 128))
    send_head(6, None, peak_buf)
    arrived(6, peak_buf)
    peak = jnp.max(peak_buf[...], axis=0)[:, 0:1]
    ratio = jnp.where(allowed, jnp.exp(scores - peak), 0.0)
    weights = ratio * jnp.clip(ratio / floor_share - 1.0, 0.0, 1.0)
    total_mine = jnp.sum(weights, axis=1, keepdims=True)
    total_buf[j] = jnp.broadcast_to(total_mine, (2, 128))
    send_head(7, None, total_buf)
    arrived(7, total_buf)
    total = jnp.sum(total_buf[...], axis=0)[:, 0:1]
    next_probs[...] = (weights / total).astype(BF)

    saves.append(save(4, next_probs, next_probs_h))
    for copy in saves:
        copy.wait()
    for phase, dst in enumerate(
        (
            group_buf,
            pair_buf,
            mixer_buf,
            mixed_buf,
            out_buf,
            None,
            peak_buf,
            total_buf,
            square_buf,
            share_buf,
            scale_buf,
            in_buf,
            *[logit_buf.at[block] for block in range(4)],
        )
    ):
        if dst is not None:
            sent(phase, dst)


def finish(*refs):
    sems = refs[-1]
    copies = [
        pltpu.make_async_copy(refs[at], refs[at + 5], sems.at[at]) for at in range(5)
    ]
    for copy in copies:
        copy.start()
    for copy in copies:
        copy.wait()


def local(
    hidden,
    norm_gain,
    input_weight,
    group_weight,
    step_weight,
    conv_inner_weight,
    conv_group_weight,
    conv_inner_state,
    conv_group_state,
    timestep_bias,
    decay_log,
    skip_gain,
    recurrent_state,
    mixer_gain,
    output_weight,
    final_gain,
    lexicon_matrix,
    token_mask,
    min_share,
):
    hbm = pl.BlockSpec(memory_space=pltpu.HBM)
    in_specs = [hbm] * N_IN
    shapes = (
            jax.ShapeDtypeStruct((2, 8, 64, 256), BF),
            jax.ShapeDtypeStruct((3, 2, 512), BF),
            jax.ShapeDtypeStruct((3, 2, 128), BF),
            jax.ShapeDtypeStruct((ROWS, 512), BF),
            jax.ShapeDtypeStruct((2, 2048), BF),
    )
    results = pl.pallas_call(
        kernel,
        out_shape=shapes,
        in_specs=in_specs,
        out_specs=(hbm,) * 5,
        scratch_shapes=[
            pltpu.VMEM((ROWS, 512), BF),
            pltpu.VMEM((512,), BF),
            pltpu.VMEM((4, 512, 2, 128), BF),
            pltpu.VMEM((512, 128), BF),
            pltpu.VMEM((8, 512), BF),
            pltpu.VMEM((4, 512), BF),
            pltpu.VMEM((4, 128), BF),
            pltpu.VMEM((3, 2, 512), BF),
            pltpu.VMEM((3, 2, 128), BF),
            pltpu.VMEM((2, 8, 64, 256), BF),
            pltpu.VMEM((512,), BF),
            pltpu.VMEM((512, 512), BF),
            pltpu.VMEM((512,), BF),
            pltpu.VMEM((512, 2048), BF),
            pltpu.VMEM((2, 2048), jnp.int32),
            pltpu.VMEM((2, 8, 64, 256), BF),
            pltpu.VMEM((3, 2, 512), BF),
            pltpu.VMEM((3, 2, 128), BF),
            pltpu.VMEM((ROWS, 512), BF),
            pltpu.VMEM((2, 2048), BF),
            pltpu.SMEM((8,), F32),
            pltpu.SMEM((8,), F32),
            pltpu.SMEM((8,), F32),
            pltpu.SMEM((2,), jnp.int32),
            pltpu.VMEM((ROWS, 1, 512), F32),
            pltpu.VMEM((NR, 1, 128), F32),
            pltpu.VMEM((NR, 2, 128), F32),
            pltpu.VMEM((NR, 2, 128), F32),
            pltpu.VMEM((NR, 2, 1152), F32),
            pltpu.VMEM((NR, 2, 1152), F32),
            pltpu.VMEM((NH, 2, 128), BF),
            pltpu.VMEM((4, 2, 128), F32),
            pltpu.VMEM((NR, 2, 512), BF),
            pltpu.VMEM((ROWS, 1, 512), F32),
            pltpu.VMEM((NH, 1, 512), F32),
            pltpu.VMEM((NR, 1, 128), F32),
            pltpu.VMEM((NH, 2, 512), BF),
            pltpu.VMEM((4, NR, 2, 512), F32),
            pltpu.VMEM((4, NR, 2, 512), F32),
            pltpu.VMEM((NH, 2, 128), F32),
            pltpu.VMEM((NH, 2, 128), F32),
            pltpu.SemaphoreType.DMA((len(SMALL),)),
            pltpu.SemaphoreType.DMA((4,)),
            pltpu.SemaphoreType.DMA((5,)),
            pltpu.SemaphoreType.DMA((16,)),
            pltpu.SemaphoreType.DMA((16,)),
        ],
        compiler_params=pltpu.CompilerParams(
            collective_id=0, has_side_effects=True, vmem_limit_bytes=56 << 20
        ),
    )(
        hidden,
        norm_gain,
        input_weight,
        group_weight,
        step_weight.T,
        conv_inner_weight,
        conv_group_weight,
        jnp.transpose(conv_inner_state, (1, 0, 2)),
        jnp.transpose(conv_group_state, (1, 0, 2)),
        timestep_bias,
        decay_log,
        skip_gain,
        recurrent_state,
        mixer_gain,
        output_weight,
        final_gain,
        lexicon_matrix,
        token_mask,
        min_share,
    )
    state, inner, group, out, probs = pl.pallas_call(
        finish,
        out_shape=shapes,
        in_specs=[hbm] * 5,
        out_specs=[hbm] * 5,
        scratch_shapes=[pltpu.SemaphoreType.DMA((5,))],
        compiler_params=pltpu.CompilerParams(vmem_limit_bytes=56 << 20),
    )(*results)
    return (
        state,
        jnp.transpose(inner, (1, 0, 2)),
        jnp.transpose(group, (1, 0, 2)),
        out,
        probs,
    )


def solution(mesh):
    in_specs = (
        P(None, "row"),
        P("row"),
        P("row", None, "head"),
        P("row", "head"),
        P("row", "head"),
        P(None, "head"),
        P(None, "head"),
        P("row", None, "head"),
        P("row", None, "head"),
        P("head"),
        P("head"),
        P("head"),
        P("row", "head", None, None),
        P("head"),
        P("head", "row"),
        P("row"),
        P("row", "head"),
        P("row", "head"),
        P("row"),
    )
    out_specs = (
        P("row", "head", None, None),
        P("row", None, "head"),
        P("row", None, "head"),
        P(None, "row"),
        P("row", "head"),
    )
    return jax.shard_map(local, mesh=mesh, in_specs=in_specs, out_specs=out_specs, check_vma=False)
```

```python
import jax
import jax.numpy as jnp
from jax import lax
from jax.experimental import pallas as pl
from jax.experimental.pallas import tpu as pltpu
from jax.sharding import PartitionSpec as P

D = 8192
HEADS = 256
HEAD_DIM = 64
STATE = 256
GROUPS = 8
NR = 16
NH = 32
ROWS = 32
EPSILON = 1e-05
INVERSE_HEAT = 1.25
FIXED_POINT = 65536.0
NEG_LARGE = -1e30
MESH = pl.DeviceIdType.MESH
BF = jnp.bfloat16
F32 = jnp.float32


def silu(v):
    return v / (1.0 + jnp.exp(-v))


def iota(shape, axis):
    return lax.broadcasted_iota(jnp.int32, shape, axis)


def dot(a, b):
    return jnp.dot(a, b, preferred_element_type=F32)


def dot_nt(a, b):
    return lax.dot_general(a, b, (((1,), (1,)), ((), ())), preferred_element_type=F32)


N_IN = 19
SMALL = (
    "hidden",
    "norm_gain",
    "group_weight",
    "step_weight",
    "conv_inner_weight",
    "conv_group_weight",
    "conv_inner_state",
    "conv_group_state",
    "mixer_gain",
    "final_gain",
    "token_mask",
    "recurrent_state",
    "output_weight",
    "lexicon_matrix",
    "timestep_bias",
    "decay_log",
    "skip_gain",
    "min_share",
)


def kernel(
    hidden_h,
    norm_gain_h,
    input_weight_h,
    group_weight_h,
    step_weight_h,
    conv_inner_weight_h,
    conv_group_weight_h,
    conv_inner_state_h,
    conv_group_state_h,
    timestep_bias_h,
    decay_log_h,
    skip_gain_h,
    recurrent_state_h,
    mixer_gain_h,
    output_weight_h,
    final_gain_h,
    lexicon_h,
    token_mask_h,
    min_share_h,
    next_state_h,
    next_conv_inner_h,
    next_conv_group_h,
    layer_out_h,
    next_probs_h,
    hidden_v,
    norm_gain_v,
    input_weight_v,
    group_weight_v,
    step_weight_v,
    conv_inner_weight_v,
    conv_group_weight_v,
    conv_inner_state_v,
    conv_group_state_v,
    recurrent_state_v,
    mixer_gain_v,
    output_weight_v,
    final_gain_v,
    lexicon_v,
    token_mask_v,
    next_state_v,
    next_conv_inner,
    next_conv_group,
    layer_out,
    next_probs,
    timestep_bias,
    decay_log,
    skip_gain,
    min_share,
    hidden_rows,
    square_buf,
    group_part,
    group_buf,
    in_part,
    in_buf,
    pair_buf,
    share_buf,
    mixer_buf,
    mixed_part,
    mixed_buf,
    scale_buf,
    out_buf,
    logit_part,
    logit_buf,
    peak_buf,
    total_buf,
    in_sem,
    weight_sem,
    save_sem,
    send_sem,
    recv_sem,
):
    i = lax.axis_index("row")
    j = lax.axis_index("head")

    barrier = pltpu.get_barrier_semaphore()

    def far_first(k, n):
        return n // 2 + (2 * (k % 2) - 1) * ((k + 1) // 2)

    def greet_row(k, carry):
        to = lax.rem(i + far_first(k, NR), NR)
        pl.semaphore_signal(barrier, inc=1, device_id=(to, j), device_id_type=MESH)
        return carry

    def greet_head(k, carry):
        to = lax.rem(j + far_first(k, NH), NH)
        pl.semaphore_signal(barrier, inc=1, device_id=(i, to), device_id_type=MESH)
        return carry

    lax.fori_loop(0, NR - 1, greet_row, 0)
    lax.fori_loop(0, NH - 1, greet_head, 0)

    loads = {
        "hidden": (hidden_h, hidden_v),
        "norm_gain": (norm_gain_h, norm_gain_v),
        "group_weight": (group_weight_h, group_weight_v),
        "step_weight": (step_weight_h, step_weight_v),
        "conv_inner_weight": (conv_inner_weight_h, conv_inner_weight_v),
        "conv_group_weight": (conv_group_weight_h, conv_group_weight_v),
        "conv_inner_state": (conv_inner_state_h, conv_inner_state_v),
        "conv_group_state": (conv_group_state_h, conv_group_state_v),
        "mixer_gain": (mixer_gain_h, mixer_gain_v),
        "final_gain": (final_gain_h, final_gain_v),
        "token_mask": (token_mask_h, token_mask_v),
        "recurrent_state": (recurrent_state_h, recurrent_state_v),
        "output_weight": (output_weight_h, output_weight_v),
        "lexicon_matrix": (lexicon_h, lexicon_v),
        "timestep_bias": (timestep_bias_h, timestep_bias),
        "decay_log": (decay_log_h, decay_log),
        "skip_gain": (skip_gain_h, skip_gain),
        "min_share": (min_share_h, min_share),
    }

    def load(name):
        src, dst = loads[name]
        return pltpu.make_async_copy(src, dst, in_sem.at[SMALL.index(name)])

    def load_weight(block):
        return pltpu.make_async_copy(
            input_weight_h.at[:, :, pl.ds(block * 128, 128)],
            input_weight_v.at[block],
            weight_sem.at[block],
        )

    load("hidden").start()
    load("norm_gain").start()
    for block in range(4):
        load_weight(block).start()
    for name in SMALL[2:]:
        load(name).start()

    def send_row(phase, src, dst):
        def step(k, carry):
            to = lax.rem(i + far_first(k, NR), NR)
            pltpu.make_async_remote_copy(
                src_ref=dst.at[i] if src is None else src.at[to],
                dst_ref=dst.at[i],
                send_sem=send_sem.at[phase],
                recv_sem=recv_sem.at[phase],
                device_id=(to, j),
                device_id_type=MESH,
            ).start()
            return carry

        lax.fori_loop(0, NR - 1, step, 0)

    def send_head(phase, src, dst):
        def step(k, carry):
            to = lax.rem(j + far_first(k, NH), NH)
            pltpu.make_async_remote_copy(
                src_ref=dst.at[j] if src is None else src.at[to],
                dst_ref=dst.at[j],
                send_sem=send_sem.at[phase],
                recv_sem=recv_sem.at[phase],
                device_id=(i, to),
                device_id_type=MESH,
            ).start()
            return carry

        lax.fori_loop(0, NH - 1, step, 0)

    def arrived(phase, dst):
        rest = dst.at[pl.ds(0, dst.shape[0] - 1)]
        pltpu.make_async_copy(rest, rest, recv_sem.at[phase]).wait()

    def sent(phase, dst):
        rest = dst.at[pl.ds(0, dst.shape[0] - 1)]
        pltpu.make_async_copy(rest, rest, send_sem.at[phase]).wait()

    def send_group(phase, dst):
        first = j - j % 4

        def step(k, carry):
            to = first + lax.rem(j + k, 4)
            pltpu.make_async_remote_copy(
                src_ref=dst.at[j % 4],
                dst_ref=dst.at[j % 4],
                send_sem=send_sem.at[phase],
                recv_sem=recv_sem.at[phase],
                device_id=(i, to),
                device_id_type=MESH,
            ).start()
            return carry

        lax.fori_loop(1, 4, step, 0)

    def save(at, src, dst):
        copy = pltpu.make_async_copy(src, dst, save_sem.at[at])
        copy.start()
        return copy

    load("hidden").wait()
    load("norm_gain").wait()
    hidden_wide = hidden_v[...].astype(F32)
    hidden_rows[:, 0, :] = hidden_wide
    squares = jnp.sum(hidden_wide * hidden_wide, axis=1, keepdims=True)
    diagonal = iota((ROWS, 128), 0) == iota((ROWS, 128), 1)
    square_buf[i] = jnp.sum(jnp.where(diagonal, squares, 0.0), axis=0, keepdims=True)
    depth_at, slot_at = iota((128, 256), 0), iota((128, 256), 1)
    spread_even = (slot_at == 2 * depth_at).astype(F32).astype(BF)
    spread_odd = (slot_at == 2 * depth_at + 1).astype(F32).astype(BF)
    load("group_weight").wait()
    pl.semaphore_wait(barrier, NR + NH - 2)
    send_row(8, None, square_buf)
    arrived(8, square_buf)
    square_total = jnp.sum(square_buf[:, 0, :], axis=0, keepdims=True)
    row_total = jnp.sum(jnp.where(diagonal, square_total, 0.0), axis=1, keepdims=True)
    hidden_scale = lax.rsqrt(row_total / D + EPSILON)

    gained = (hidden_wide * hidden_scale * norm_gain_v[...].astype(F32).reshape(1, 512)).astype(BF)
    group_part[...] = dot(gained, group_weight_v[...]).reshape(NR, 2, 128)
    send_row(0, group_part, group_buf)
    group_buf[i] = group_part[i]
    blocks = [gained[:, 128 * b : 128 * b + 128] for b in range(4)]
    doubled = jnp.concatenate(
        [
            jnp.concatenate([dot(part, spread_even) for part in blocks], axis=1),
            jnp.concatenate([dot(part, spread_odd) for part in blocks], axis=1),
        ],
        axis=0,
    ).astype(BF)
    for block in range(4):
        load_weight(block).wait()
        both = dot(doubled, input_weight_v[block].reshape(1024, 128))
        in_part[:, :, 128 * block : 128 * block + 128] = both[:32].reshape(NR, 2, 128)
        in_part[:, :, 512 + 128 * block : 640 + 128 * block] = both[32:].reshape(NR, 2, 128)
    load("step_weight").wait()
    step_rows = jnp.concatenate(
        [step_weight_v[...].astype(F32), jnp.zeros((120, 512), F32)], axis=0
    ).astype(BF)
    in_part[:, :, 1024:1152] = dot_nt(gained, step_rows).reshape(NR, 2, 128)
    send_row(11, in_part, in_buf)
    in_buf[i] = in_part[i]

    for name in ("conv_inner_weight", "conv_group_weight", "conv_inner_state", "conv_group_state"):
        load(name).wait()
    arrived(0, group_buf)
    group_new = jnp.sum(group_buf[...], axis=0).astype(BF)
    group_old = conv_group_state_v[...].astype(F32)
    group_taps = conv_group_weight_v[...].astype(F32)
    group_mix = (
        group_old[0] * group_taps[0:1]
        + group_old[1] * group_taps[1:2]
        + group_old[2] * group_taps[2:3]
        + group_new.astype(F32) * group_taps[3:4]
    )
    pair_buf[j] = silu(group_mix).astype(BF)
    send_head(1, None, pair_buf)

    next_conv_group[0] = conv_group_state_v[1]
    next_conv_group[1] = conv_group_state_v[2]
    next_conv_group[2] = group_new
    arrived(11, in_buf)
    projected = jnp.sum(in_buf[...], axis=0)
    inner_new = projected[:, 512:1024].astype(BF)
    next_conv_inner[0] = conv_inner_state_v[1]
    next_conv_inner[1] = conv_inner_state_v[2]
    next_conv_inner[2] = inner_new
    inner_old = conv_inner_state_v[...].astype(F32)
    inner_taps = conv_inner_weight_v[...].astype(F32)
    conv_inner = silu(
        inner_old[0] * inner_taps[0:1]
        + inner_old[1] * inner_taps[1:2]
        + inner_old[2] * inner_taps[2:3]
        + inner_new.astype(F32) * inner_taps[3:4]
    )
    gate = silu(projected[:, :512])
    step_raw = projected[:, 1024:1032]
    saves = [
        save(1, next_conv_inner, next_conv_inner_h),
        save(2, next_conv_group, next_conv_group_h),
    ]
    for name in ("timestep_bias", "decay_log", "skip_gain"):
        load(name).wait()
    head_of = iota((2, 512), 1) // HEAD_DIM
    step_in = jnp.zeros((2, 512), F32)
    rate_log = jnp.zeros((2, 512), F32)
    skip = jnp.zeros((2, 512), F32)
    for h in range(8):
        here = head_of == h
        step_in = jnp.where(here, step_raw[:, h : h + 1] + timestep_bias[h], step_in)
        rate_log = jnp.where(here, decay_log[h], rate_log)
        skip = jnp.where(here, skip_gain[h], skip)
    step_size = jnp.maximum(step_in, 0.0) + jnp.log1p(jnp.exp(-jnp.abs(step_in)))
    decay = jnp.exp(-step_size * jnp.exp(rate_log))
    driven = step_size * conv_inner

    group_at = j // (NH // GROUPS)
    channel_at, entry_at = iota((128, 256), 0), iota((128, 256), 1)
    pick = (channel_at == (entry_at % 16) * GROUPS + group_at).astype(F32).astype(BF)
    source_at, entry_of = iota((NH, 256), 0), iota((NH, 256), 1) // 16
    load("recurrent_state").wait()
    load("mixer_gain").wait()
    arrived(1, pair_buf)
    inputs, readouts = [], []
    for r in range(2):
        picked = dot(pair_buf[:, r, :], pick)
        inputs.append(
            jnp.sum(jnp.where(source_at == entry_of, picked, 0.0), axis=0, keepdims=True)
        )
        readouts.append(
            jnp.sum(jnp.where(source_at == entry_of + 16, picked, 0.0), axis=0, keepdims=True)
        )
    readout = []
    for r in range(2):
        old_read = dot_nt(readouts[r].astype(BF), recurrent_state_v[r].reshape(512, 256))
        pair_dot = jnp.sum(inputs[r] * readouts[r], axis=1, keepdims=True)
        readout.append(
            decay[r : r + 1] * old_read
            + driven[r : r + 1] * pair_dot
            + skip[r : r + 1] * conv_inner[r : r + 1]
        )
    gated = jnp.concatenate(readout, axis=0) * gate
    gated_squares = jnp.sum(gated * gated, axis=1, keepdims=True)
    mixer_gain_wide = mixer_gain_v[...].astype(F32).reshape(1, 512)
    share_buf[j % 4] = jnp.broadcast_to(gated_squares, (2, 128))
    send_group(9, share_buf)
    arrived(9, share_buf)
    group_total = jnp.sum(share_buf[...], axis=0)[:, 0:1]
    group_scale = lax.rsqrt(group_total / (HEADS * HEAD_DIM // GROUPS) + EPSILON)
    mixer_buf[i] = (gated * group_scale * mixer_gain_wide).astype(BF)
    send_row(2, None, mixer_buf)

    rows8 = jnp.concatenate([driven, decay, jnp.zeros((4, 512), F32)], axis=0)
    columns = rows8.T
    for r in range(2):
        for h in range(8):
            at = slice(64 * h, 64 * h + 64)
            fresh = (
                columns[at, 2 + r : 3 + r] * recurrent_state_v[r, h].astype(F32)
                + columns[at, r : r + 1] * inputs[r]
            )
            next_state_v[r, h] = fresh.astype(BF)
    saves.append(save(0, next_state_v, next_state_h))

    load("output_weight").wait()
    arrived(2, mixer_buf)
    mixer_rows = mixer_buf[...].reshape(ROWS, 512)
    mixed_part[:, 0, :] = dot(mixer_rows, output_weight_v[...])
    send_head(3, mixed_part, mixed_buf)
    mixed_buf[j] = mixed_part[j]

    load("final_gain").wait()
    final_gain_wide = final_gain_v[...].astype(F32).reshape(1, 512)
    arrived(3, mixed_buf)
    mixed = jnp.sum(mixed_buf[:, 0, :], axis=0, keepdims=True)
    out_rounded = (hidden_rows[j] + mixed).astype(BF)
    out_mine = out_rounded.astype(F32)
    scale_buf[i] = jnp.broadcast_to(jnp.sum(out_mine * out_mine, axis=1, keepdims=True), (1, 128))
    send_row(10, None, scale_buf)
    arrived(10, scale_buf)
    out_total = jnp.sum(scale_buf[:, 0, :], axis=0, keepdims=True)[:, 0:1]
    out_scale = lax.rsqrt(out_total / D + EPSILON)
    final_mine = (out_mine * out_scale * final_gain_wide).astype(BF).astype(F32)
    out_buf[j] = jnp.concatenate([final_mine, out_mine], axis=0).astype(BF)
    send_head(4, None, out_buf)

    load("lexicon_matrix").wait()
    load("token_mask").wait()
    load("min_share").wait()
    arrived(4, out_buf)
    final_rows = out_buf[:, 0, :]
    for block in range(4):
        at = slice(512 * block, 512 * block + 512)
        logit_part[block] = dot(final_rows, lexicon_v[:, at]).reshape(NR, 2, 512)
        send_row(12 + block, logit_part.at[block], logit_buf.at[block])
        logit_buf[block, i] = logit_part[block, i]
    layer_out[...] = out_buf[:, 1, :]
    saves.append(save(3, layer_out, layer_out_h))

    allowed = token_mask_v[...] > 0
    row_at = iota((2, 1), 0)
    floor_share = (
        jnp.where(row_at == 0, min_share[0], min_share[1]).astype(F32) / FIXED_POINT
    )
    sums = []
    for block in range(4):
        arrived(12 + block, logit_buf.at[block])
        sums.append(jnp.sum(logit_buf[block], axis=0))
    scores = jnp.concatenate(sums, axis=1) * INVERSE_HEAT
    peak_mine = jnp.max(jnp.where(allowed, scores, NEG_LARGE), axis=1, keepdims=True)
    peak_buf[j] = jnp.broadcast_to(peak_mine, (2, 128))
    send_head(6, None, peak_buf)
    arrived(6, peak_buf)
    peak = jnp.max(peak_buf[...], axis=0)[:, 0:1]
    ratio = jnp.where(allowed, jnp.exp(scores - peak), 0.0)
    weights = ratio * jnp.clip(ratio / floor_share - 1.0, 0.0, 1.0)
    total_mine = jnp.sum(weights, axis=1, keepdims=True)
    total_buf[j] = jnp.broadcast_to(total_mine, (2, 128))
    send_head(7, None, total_buf)
    arrived(7, total_buf)
    total = jnp.sum(total_buf[...], axis=0)[:, 0:1]
    next_probs[...] = (weights / total).astype(BF)

    saves.append(save(4, next_probs, next_probs_h))
    for copy in saves:
        copy.wait()
    for phase, dst in enumerate(
        (
            group_buf,
            pair_buf,
            mixer_buf,
            mixed_buf,
            out_buf,
            None,
            peak_buf,
            total_buf,
            square_buf,
            share_buf,
            scale_buf,
            in_buf,
            *[logit_buf.at[block] for block in range(4)],
        )
    ):
        if dst is not None:
            sent(phase, dst)


def finish(*refs):
    sems = refs[-1]
    copies = [
        pltpu.make_async_copy(refs[at], refs[at + 5], sems.at[at]) for at in range(5)
    ]
    for copy in copies:
        copy.start()
    for copy in copies:
        copy.wait()


def local(
    hidden,
    norm_gain,
    input_weight,
    group_weight,
    step_weight,
    conv_inner_weight,
    conv_group_weight,
    conv_inner_state,
    conv_group_state,
    timestep_bias,
    decay_log,
    skip_gain,
    recurrent_state,
    mixer_gain,
    output_weight,
    final_gain,
    lexicon_matrix,
    token_mask,
    min_share,
):
    hbm = pl.BlockSpec(memory_space=pltpu.HBM)
    in_specs = [hbm] * N_IN
    shapes = (
            jax.ShapeDtypeStruct((2, 8, 64, 256), BF),
            jax.ShapeDtypeStruct((3, 2, 512), BF),
            jax.ShapeDtypeStruct((3, 2, 128), BF),
            jax.ShapeDtypeStruct((ROWS, 512), BF),
            jax.ShapeDtypeStruct((2, 2048), BF),
    )
    results = pl.pallas_call(
        kernel,
        out_shape=tuple(pltpu.VMEM(shape.shape, BF) for shape in shapes),
        in_specs=in_specs,
        out_specs=(pl.BlockSpec(memory_space=pltpu.VMEM),) * 5,
        scratch_shapes=[
            pltpu.VMEM((ROWS, 512), BF),
            pltpu.VMEM((512,), BF),
            pltpu.VMEM((4, 512, 2, 128), BF),
            pltpu.VMEM((512, 128), BF),
            pltpu.VMEM((8, 512), BF),
            pltpu.VMEM((4, 512), BF),
            pltpu.VMEM((4, 128), BF),
            pltpu.VMEM((3, 2, 512), BF),
            pltpu.VMEM((3, 2, 128), BF),
            pltpu.VMEM((2, 8, 64, 256), BF),
            pltpu.VMEM((512,), BF),
            pltpu.VMEM((512, 512), BF),
            pltpu.VMEM((512,), BF),
            pltpu.VMEM((512, 2048), BF),
            pltpu.VMEM((2, 2048), jnp.int32),
            pltpu.VMEM((2, 8, 64, 256), BF),
            pltpu.VMEM((3, 2, 512), BF),
            pltpu.VMEM((3, 2, 128), BF),
            pltpu.VMEM((ROWS, 512), BF),
            pltpu.VMEM((2, 2048), BF),
            pltpu.SMEM((8,), F32),
            pltpu.SMEM((8,), F32),
            pltpu.SMEM((8,), F32),
            pltpu.SMEM((2,), jnp.int32),
            pltpu.VMEM((ROWS, 1, 512), F32),
            pltpu.VMEM((NR, 1, 128), F32),
            pltpu.VMEM((NR, 2, 128), F32),
            pltpu.VMEM((NR, 2, 128), F32),
            pltpu.VMEM((NR, 2, 1152), F32),
            pltpu.VMEM((NR, 2, 1152), F32),
            pltpu.VMEM((NH, 2, 128), BF),
            pltpu.VMEM((4, 2, 128), F32),
            pltpu.VMEM((NR, 2, 512), BF),
            pltpu.VMEM((ROWS, 1, 512), F32),
            pltpu.VMEM((NH, 1, 512), F32),
            pltpu.VMEM((NR, 1, 128), F32),
            pltpu.VMEM((NH, 2, 512), BF),
            pltpu.VMEM((4, NR, 2, 512), F32),
            pltpu.VMEM((4, NR, 2, 512), F32),
            pltpu.VMEM((NH, 2, 128), F32),
            pltpu.VMEM((NH, 2, 128), F32),
            pltpu.SemaphoreType.DMA((len(SMALL),)),
            pltpu.SemaphoreType.DMA((4,)),
            pltpu.SemaphoreType.DMA((5,)),
            pltpu.SemaphoreType.DMA((16,)),
            pltpu.SemaphoreType.DMA((16,)),
        ],
        compiler_params=pltpu.CompilerParams(
            collective_id=0, has_side_effects=True, vmem_limit_bytes=56 << 20
        ),
    )(
        hidden,
        norm_gain,
        input_weight,
        group_weight,
        step_weight.T,
        conv_inner_weight,
        conv_group_weight,
        jnp.transpose(conv_inner_state, (1, 0, 2)),
        jnp.transpose(conv_group_state, (1, 0, 2)),
        timestep_bias,
        decay_log,
        skip_gain,
        recurrent_state,
        mixer_gain,
        output_weight,
        final_gain,
        lexicon_matrix,
        token_mask,
        min_share,
    )
    state, inner, group, out, probs = pl.pallas_call(
        finish,
        out_shape=shapes,
        in_specs=[pl.BlockSpec(memory_space=pltpu.VMEM)] * 5,
        out_specs=[hbm] * 5,
        scratch_shapes=[pltpu.SemaphoreType.DMA((5,))],
        compiler_params=pltpu.CompilerParams(vmem_limit_bytes=1 << 20),
    )(*results)
    return (
        state,
        jnp.transpose(inner, (1, 0, 2)),
        jnp.transpose(group, (1, 0, 2)),
        out,
        probs,
    )


def solution(mesh):
    in_specs = (
        P(None, "row"),
        P("row"),
        P("row", None, "head"),
        P("row", "head"),
        P("row", "head"),
        P(None, "head"),
        P(None, "head"),
        P("row", None, "head"),
        P("row", None, "head"),
        P("head"),
        P("head"),
        P("head"),
        P("row", "head", None, None),
        P("head"),
        P("head", "row"),
        P("row"),
        P("row", "head"),
        P("row", "head"),
        P("row"),
    )
    out_specs = (
        P("row", "head", None, None),
        P("row", None, "head"),
        P("row", None, "head"),
        P(None, "row"),
        P("row", "head"),
    )
    return jax.shard_map(local, mesh=mesh, in_specs=in_specs, out_specs=out_specs, check_vma=False)
```

```python
import jax
import jax.numpy as jnp
from jax import lax
from jax.experimental import pallas as pl
from jax.experimental.pallas import tpu as pltpu
from jax.sharding import PartitionSpec as P

D = 8192
HEADS = 256
HEAD_DIM = 64
STATE = 256
GROUPS = 8
NR = 16
NH = 32
ROWS = 32
EPSILON = 1e-05
INVERSE_HEAT = 1.25
FIXED_POINT = 65536.0
NEG_LARGE = -1e30
MESH = pl.DeviceIdType.MESH
BF = jnp.bfloat16
F32 = jnp.float32


def silu(v):
    return v / (1.0 + jnp.exp(-v))


def iota(shape, axis):
    return lax.broadcasted_iota(jnp.int32, shape, axis)


def dot(a, b):
    return jnp.dot(a, b, preferred_element_type=F32)


def dot_nt(a, b):
    return lax.dot_general(a, b, (((1,), (1,)), ((), ())), preferred_element_type=F32)


N_IN = 19
SMALL = (
    "hidden",
    "norm_gain",
    "group_weight",
    "step_weight",
    "conv_inner_weight",
    "conv_group_weight",
    "conv_inner_state",
    "conv_group_state",
    "mixer_gain",
    "final_gain",
    "token_mask",
    "recurrent_state",
    "output_weight",
    "lexicon_matrix",
    "timestep_bias",
    "decay_log",
    "skip_gain",
    "min_share",
)


def kernel(
    hidden_h,
    norm_gain_h,
    input_weight_h,
    group_weight_h,
    step_weight_h,
    conv_inner_weight_h,
    conv_group_weight_h,
    conv_inner_state_h,
    conv_group_state_h,
    timestep_bias_h,
    decay_log_h,
    skip_gain_h,
    recurrent_state_h,
    mixer_gain_h,
    output_weight_h,
    final_gain_h,
    lexicon_h,
    token_mask_h,
    min_share_h,
    next_state_h,
    next_conv_inner_h,
    next_conv_group_h,
    layer_out_h,
    next_probs_h,
    hidden_v,
    norm_gain_v,
    input_weight_v,
    group_weight_v,
    step_weight_v,
    conv_inner_weight_v,
    conv_group_weight_v,
    conv_inner_state_v,
    conv_group_state_v,
    recurrent_state_v,
    mixer_gain_v,
    output_weight_v,
    final_gain_v,
    lexicon_v,
    token_mask_v,
    next_state_v,
    next_conv_inner,
    next_conv_group,
    layer_out,
    next_probs,
    timestep_bias,
    decay_log,
    skip_gain,
    min_share,
    hidden_rows,
    square_buf,
    group_part,
    group_buf,
    in_part,
    in_buf,
    pair_buf,
    share_buf,
    mixer_buf,
    mixed_part,
    mixed_buf,
    scale_buf,
    out_buf,
    norm_buf,
    logit_part,
    logit_buf,
    rest_part,
    rest_buf,
    main_rest,
    peak_buf,
    total_buf,
    in_sem,
    weight_sem,
    save_sem,
    send_sem,
    recv_sem,
):
    i = lax.axis_index("row")
    j = lax.axis_index("head")

    barrier = pltpu.get_barrier_semaphore()

    def far_first(k, n):
        return n // 2 + (2 * (k % 2) - 1) * ((k + 1) // 2)

    def greet_row(k, carry):
        to = lax.rem(i + far_first(k, NR), NR)
        pl.semaphore_signal(barrier, inc=1, device_id=(to, j), device_id_type=MESH)
        return carry

    def greet_head(k, carry):
        to = lax.rem(j + far_first(k, NH), NH)
        pl.semaphore_signal(barrier, inc=1, device_id=(i, to), device_id_type=MESH)
        return carry

    lax.fori_loop(0, NR - 1, greet_row, 0)
    lax.fori_loop(0, NH - 1, greet_head, 0)

    loads = {
        "hidden": (hidden_h, hidden_v),
        "norm_gain": (norm_gain_h, norm_gain_v),
        "group_weight": (group_weight_h, group_weight_v),
        "step_weight": (step_weight_h, step_weight_v),
        "conv_inner_weight": (conv_inner_weight_h, conv_inner_weight_v),
        "conv_group_weight": (conv_group_weight_h, conv_group_weight_v),
        "conv_inner_state": (conv_inner_state_h, conv_inner_state_v),
        "conv_group_state": (conv_group_state_h, conv_group_state_v),
        "mixer_gain": (mixer_gain_h, mixer_gain_v),
        "final_gain": (final_gain_h, final_gain_v),
        "token_mask": (token_mask_h, token_mask_v),
        "recurrent_state": (recurrent_state_h, recurrent_state_v),
        "output_weight": (output_weight_h, output_weight_v),
        "lexicon_matrix": (lexicon_h, lexicon_v),
        "timestep_bias": (timestep_bias_h, timestep_bias),
        "decay_log": (decay_log_h, decay_log),
        "skip_gain": (skip_gain_h, skip_gain),
        "min_share": (min_share_h, min_share),
    }

    def load(name):
        src, dst = loads[name]
        return pltpu.make_async_copy(src, dst, in_sem.at[SMALL.index(name)])

    def load_weight(block):
        return pltpu.make_async_copy(
            input_weight_h.at[:, :, pl.ds(block * 128, 128)],
            input_weight_v.at[block],
            weight_sem.at[block],
        )

    load("hidden").start()
    load("norm_gain").start()
    for block in range(4):
        load_weight(block).start()
    for name in SMALL[2:]:
        load(name).start()

    def send_row(phase, src, dst):
        def step(k, carry):
            to = lax.rem(i + far_first(k, NR), NR)
            pltpu.make_async_remote_copy(
                src_ref=dst.at[i] if src is None else src.at[to],
                dst_ref=dst.at[i],
                send_sem=send_sem.at[phase],
                recv_sem=recv_sem.at[phase],
                device_id=(to, j),
                device_id_type=MESH,
            ).start()
            return carry

        lax.fori_loop(0, NR - 1, step, 0)

    def send_head(phase, src, dst):
        def step(k, carry):
            to = lax.rem(j + far_first(k, NH), NH)
            pltpu.make_async_remote_copy(
                src_ref=dst.at[j] if src is None else src.at[to],
                dst_ref=dst.at[j],
                send_sem=send_sem.at[phase],
                recv_sem=recv_sem.at[phase],
                device_id=(i, to),
                device_id_type=MESH,
            ).start()
            return carry

        lax.fori_loop(0, NH - 1, step, 0)

    def arrived(phase, dst):
        rest = dst.at[pl.ds(0, dst.shape[0] - 1)]
        pltpu.make_async_copy(rest, rest, recv_sem.at[phase]).wait()

    def sent(phase, dst):
        rest = dst.at[pl.ds(0, dst.shape[0] - 1)]
        pltpu.make_async_copy(rest, rest, send_sem.at[phase]).wait()

    def send_group(phase, dst):
        first = j - j % 4

        def step(k, carry):
            to = first + lax.rem(j + k, 4)
            pltpu.make_async_remote_copy(
                src_ref=dst.at[j % 4],
                dst_ref=dst.at[j % 4],
                send_sem=send_sem.at[phase],
                recv_sem=recv_sem.at[phase],
                device_id=(i, to),
                device_id_type=MESH,
            ).start()
            return carry

        lax.fori_loop(1, 4, step, 0)

    def save(at, src, dst):
        copy = pltpu.make_async_copy(src, dst, save_sem.at[at])
        copy.start()
        return copy

    load("hidden").wait()
    load("norm_gain").wait()
    hidden_wide = hidden_v[...].astype(F32)
    hidden_rows[:, 0, :] = hidden_wide
    squares = jnp.sum(hidden_wide * hidden_wide, axis=1, keepdims=True)
    diagonal = iota((ROWS, 128), 0) == iota((ROWS, 128), 1)
    square_buf[i] = jnp.sum(jnp.where(diagonal, squares, 0.0), axis=0, keepdims=True)
    depth_at, slot_at = iota((128, 256), 0), iota((128, 256), 1)
    spread_even = (slot_at == 2 * depth_at).astype(F32).astype(BF)
    spread_odd = (slot_at == 2 * depth_at + 1).astype(F32).astype(BF)
    load("group_weight").wait()
    pl.semaphore_wait(barrier, NR + NH - 2)
    send_row(8, None, square_buf)
    arrived(8, square_buf)
    square_total = jnp.sum(square_buf[...], axis=0)
    row_total = jnp.sum(jnp.where(diagonal, square_total, 0.0), axis=1, keepdims=True)
    hidden_scale = lax.rsqrt(row_total / D + EPSILON)

    gained = (hidden_wide * hidden_scale * norm_gain_v[...].astype(F32).reshape(1, 512)).astype(BF)
    group_part[...] = dot(gained, group_weight_v[...]).reshape(NR, 2, 128)
    send_row(0, group_part, group_buf)
    group_buf[i] = group_part[i]
    blocks = [gained[:, 128 * b : 128 * b + 128] for b in range(4)]
    doubled = jnp.concatenate(
        [
            jnp.concatenate([dot(part, spread_even) for part in blocks], axis=1),
            jnp.concatenate([dot(part, spread_odd) for part in blocks], axis=1),
        ],
        axis=0,
    ).astype(BF)
    for block in range(4):
        load_weight(block).wait()
        both = dot(doubled, input_weight_v[block].reshape(1024, 128))
        in_part[:, :, 128 * block : 128 * block + 128] = both[:32].reshape(NR, 2, 128)
        in_part[:, :, 512 + 128 * block : 640 + 128 * block] = both[32:].reshape(NR, 2, 128)
    load("step_weight").wait()
    step_rows = jnp.concatenate(
        [step_weight_v[...].astype(F32), jnp.zeros((120, 512), F32)], axis=0
    ).astype(BF)
    in_part[:, :, 1024:1152] = dot_nt(gained, step_rows).reshape(NR, 2, 128)
    send_row(11, in_part, in_buf)
    in_buf[i] = in_part[i]

    for name in ("conv_inner_weight", "conv_group_weight", "conv_inner_state", "conv_group_state"):
        load(name).wait()
    arrived(0, group_buf)
    group_new = jnp.sum(group_buf[...], axis=0).astype(BF)
    group_old = conv_group_state_v[...].astype(F32)
    group_taps = conv_group_weight_v[...].astype(F32)
    group_mix = (
        group_old[0] * group_taps[0:1]
        + group_old[1] * group_taps[1:2]
        + group_old[2] * group_taps[2:3]
        + group_new.astype(F32) * group_taps[3:4]
    )
    pair_buf[j] = silu(group_mix).astype(BF)
    send_head(1, None, pair_buf)

    next_conv_group[0] = conv_group_state_v[1]
    next_conv_group[1] = conv_group_state_v[2]
    next_conv_group[2] = group_new
    arrived(11, in_buf)
    projected = jnp.sum(in_buf[...], axis=0)
    inner_new = projected[:, 512:1024].astype(BF)
    next_conv_inner[0] = conv_inner_state_v[1]
    next_conv_inner[1] = conv_inner_state_v[2]
    next_conv_inner[2] = inner_new
    inner_old = conv_inner_state_v[...].astype(F32)
    inner_taps = conv_inner_weight_v[...].astype(F32)
    conv_inner = silu(
        inner_old[0] * inner_taps[0:1]
        + inner_old[1] * inner_taps[1:2]
        + inner_old[2] * inner_taps[2:3]
        + inner_new.astype(F32) * inner_taps[3:4]
    )
    gate = silu(projected[:, :512])
    step_raw = projected[:, 1024:1032]
    saves = [
        save(1, next_conv_inner, next_conv_inner_h),
        save(2, next_conv_group, next_conv_group_h),
    ]
    for name in ("timestep_bias", "decay_log", "skip_gain"):
        load(name).wait()
    head_of = iota((2, 512), 1) // HEAD_DIM
    step_in = jnp.zeros((2, 512), F32)
    rate_log = jnp.zeros((2, 512), F32)
    skip = jnp.zeros((2, 512), F32)
    for h in range(8):
        here = head_of == h
        step_in = jnp.where(here, step_raw[:, h : h + 1] + timestep_bias[h], step_in)
        rate_log = jnp.where(here, decay_log[h], rate_log)
        skip = jnp.where(here, skip_gain[h], skip)
    step_size = jnp.maximum(step_in, 0.0) + jnp.log1p(jnp.exp(-jnp.abs(step_in)))
    decay = jnp.exp(-step_size * jnp.exp(rate_log))
    driven = step_size * conv_inner

    group_at = j // (NH // GROUPS)
    channel_at, entry_at = iota((128, 256), 0), iota((128, 256), 1)
    pick = (channel_at == (entry_at % 16) * GROUPS + group_at).astype(F32).astype(BF)
    source_at, entry_of = iota((NH, 256), 0), iota((NH, 256), 1) // 16
    load("recurrent_state").wait()
    load("mixer_gain").wait()
    arrived(1, pair_buf)
    inputs, readouts = [], []
    for r in range(2):
        picked = dot(pair_buf[:, r, :], pick)
        inputs.append(
            jnp.sum(jnp.where(source_at == entry_of, picked, 0.0), axis=0, keepdims=True)
        )
        readouts.append(
            jnp.sum(jnp.where(source_at == entry_of + 16, picked, 0.0), axis=0, keepdims=True)
        )
    readout = []
    for r in range(2):
        old_read = dot_nt(readouts[r].astype(BF), recurrent_state_v[r].reshape(512, 256))
        pair_dot = jnp.sum(inputs[r] * readouts[r], axis=1, keepdims=True)
        readout.append(
            decay[r : r + 1] * old_read
            + driven[r : r + 1] * pair_dot
            + skip[r : r + 1] * conv_inner[r : r + 1]
        )
    gated = jnp.concatenate(readout, axis=0) * gate
    gated_squares = jnp.sum(gated * gated, axis=1, keepdims=True)
    mixer_gain_wide = mixer_gain_v[...].astype(F32).reshape(1, 512)
    share_buf[j % 4] = jnp.broadcast_to(gated_squares, (2, 128))
    send_group(9, share_buf)
    arrived(9, share_buf)
    group_total = jnp.sum(share_buf[...], axis=0)[:, 0:1]
    group_scale = lax.rsqrt(group_total / (HEADS * HEAD_DIM // GROUPS) + EPSILON)
    mixer_buf[i] = (gated * group_scale * mixer_gain_wide).astype(BF)
    send_row(2, None, mixer_buf)

    rows8 = jnp.concatenate([driven, decay, jnp.zeros((4, 512), F32)], axis=0)
    columns = rows8.T
    for r in range(2):
        for h in range(8):
            at = slice(64 * h, 64 * h + 64)
            fresh = (
                columns[at, 2 + r : 3 + r] * recurrent_state_v[r, h].astype(F32)
                + columns[at, r : r + 1] * inputs[r]
            )
            next_state_v[r, h] = fresh.astype(BF)
    saves.append(save(0, next_state_v, next_state_h))

    load("output_weight").wait()
    arrived(2, mixer_buf)
    mixer_rows = mixer_buf[...].reshape(ROWS, 512)
    mixed_part[:, 0, :] = dot(mixer_rows, output_weight_v[...])
    send_head(3, mixed_part, mixed_buf)
    mixed_buf[j] = mixed_part[j]

    load("final_gain").wait()
    final_gain_wide = final_gain_v[...].astype(F32).reshape(1, 512)
    arrived(3, mixed_buf)
    mixed = jnp.sum(mixed_buf[...], axis=0)
    out_mine = (hidden_rows[j] + mixed).astype(BF).astype(F32)
    scale_buf[i] = jnp.broadcast_to(jnp.sum(out_mine * out_mine, axis=1, keepdims=True), (1, 128))
    send_row(10, None, scale_buf)
    out_buf[j] = out_mine
    send_head(4, None, out_buf)
    arrived(10, scale_buf)
    norm_buf[j] = lax.rsqrt(jnp.sum(scale_buf[...], axis=0) / D + EPSILON)
    send_head(5, None, norm_buf)

    load("lexicon_matrix").wait()
    load("token_mask").wait()
    load("min_share").wait()
    arrived(4, out_buf)
    out_wide = out_buf[:, 0, :]
    scaled = out_wide * final_gain_wide
    upper = scaled.astype(BF)
    lower = (scaled - upper.astype(F32)).astype(BF)
    exact_rows = jnp.concatenate([upper, lower], axis=0)
    for block in range(2):
        both = dot(exact_rows, lexicon_v[:, 1024 * block : 1024 * block + 1024])
        main = both[:ROWS] + both[ROWS:]
        coarse = main.astype(BF)
        main_rest[block] = main - coarse.astype(F32)
        logit_part[block] = coarse.reshape(NR, 2, 1024)
        send_row(12 + block, logit_part.at[block], logit_buf.at[block])
        logit_buf[block, i] = logit_part[block, i]
    layer_out[...] = out_wide.astype(BF)
    saves.append(save(3, layer_out, layer_out_h))

    arrived(5, norm_buf)
    row_scale = norm_buf[:, 0, :][:, 0:1]
    normed_out = out_wide * row_scale * final_gain_wide
    rounding = (normed_out.astype(BF).astype(F32) - normed_out).astype(BF)
    for block in range(2):
        rest = dot(rounding, lexicon_v[:, 1024 * block : 1024 * block + 1024])
        rest = (rest + main_rest[block] * row_scale).astype(BF)
        rest_part[block] = rest.reshape(NR, 2, 1024)
        send_row(14 + block, rest_part.at[block], rest_buf.at[block])
        rest_buf[block, i] = rest_part[block, i]
    scale_mine = jnp.concatenate([norm_buf[2 * i], norm_buf[2 * i + 1]], axis=0)[:, 0:1]

    allowed = token_mask_v[...] > 0
    row_at = iota((2, 1), 0)
    floor_share = (
        jnp.where(row_at == 0, min_share[0], min_share[1]).astype(F32) / FIXED_POINT
    )
    sums = []
    for block in range(2):
        arrived(12 + block, logit_buf.at[block])
        sums.append(jnp.sum(logit_buf[block].astype(F32), axis=0) * scale_mine)
    for block in range(2):
        arrived(14 + block, rest_buf.at[block])
        sums[block] += jnp.sum(rest_buf[block].astype(F32), axis=0)
    scores = jnp.concatenate(sums, axis=1) * INVERSE_HEAT
    peak_mine = jnp.max(jnp.where(allowed, scores, NEG_LARGE), axis=1, keepdims=True)
    peak_buf[j] = jnp.broadcast_to(peak_mine, (2, 128))
    send_head(6, None, peak_buf)
    arrived(6, peak_buf)
    peak = jnp.max(peak_buf[...], axis=0)[:, 0:1]
    ratio = jnp.where(allowed, jnp.exp(scores - peak), 0.0)
    weights = ratio * jnp.clip(ratio / floor_share - 1.0, 0.0, 1.0)
    total_mine = jnp.sum(weights, axis=1, keepdims=True)
    total_buf[j] = jnp.broadcast_to(total_mine, (2, 128))
    send_head(7, None, total_buf)
    arrived(7, total_buf)
    total = jnp.sum(total_buf[...], axis=0)[:, 0:1]
    next_probs[...] = (weights / total).astype(BF)

    saves.append(save(4, next_probs, next_probs_h))
    for copy in saves:
        copy.wait()
    for phase, dst in enumerate(
        (
            group_buf,
            pair_buf,
            mixer_buf,
            mixed_buf,
            out_buf,
            norm_buf,
            peak_buf,
            total_buf,
            square_buf,
            share_buf,
            scale_buf,
            in_buf,
            *[logit_buf.at[block] for block in range(2)],
            *[rest_buf.at[block] for block in range(2)],
        )
    ):
        sent(phase, dst)


def finish(*refs):
    sems = refs[-1]
    copies = [
        pltpu.make_async_copy(refs[at], refs[at + 5], sems.at[at]) for at in range(5)
    ]
    for copy in copies:
        copy.start()
    for copy in copies:
        copy.wait()


def local(
    hidden,
    norm_gain,
    input_weight,
    group_weight,
    step_weight,
    conv_inner_weight,
    conv_group_weight,
    conv_inner_state,
    conv_group_state,
    timestep_bias,
    decay_log,
    skip_gain,
    recurrent_state,
    mixer_gain,
    output_weight,
    final_gain,
    lexicon_matrix,
    token_mask,
    min_share,
):
    hbm = pl.BlockSpec(memory_space=pltpu.HBM)
    in_specs = [hbm] * N_IN
    shapes = (
            jax.ShapeDtypeStruct((2, 8, 64, 256), BF),
            jax.ShapeDtypeStruct((3, 2, 512), BF),
            jax.ShapeDtypeStruct((3, 2, 128), BF),
            jax.ShapeDtypeStruct((ROWS, 512), BF),
            jax.ShapeDtypeStruct((2, 2048), BF),
    )
    results = pl.pallas_call(
        kernel,
        out_shape=tuple(pltpu.VMEM(shape.shape, BF) for shape in shapes),
        in_specs=in_specs,
        out_specs=(pl.BlockSpec(memory_space=pltpu.VMEM),) * 5,
        scratch_shapes=[
            pltpu.VMEM((ROWS, 512), BF),
            pltpu.VMEM((512,), BF),
            pltpu.VMEM((4, 512, 2, 128), BF),
            pltpu.VMEM((512, 128), BF),
            pltpu.VMEM((8, 512), BF),
            pltpu.VMEM((4, 512), BF),
            pltpu.VMEM((4, 128), BF),
            pltpu.VMEM((3, 2, 512), BF),
            pltpu.VMEM((3, 2, 128), BF),
            pltpu.VMEM((2, 8, 64, 256), BF),
            pltpu.VMEM((512,), BF),
            pltpu.VMEM((512, 512), BF),
            pltpu.VMEM((512,), BF),
            pltpu.VMEM((512, 2048), BF),
            pltpu.VMEM((2, 2048), jnp.int32),
            pltpu.VMEM((2, 8, 64, 256), BF),
            pltpu.VMEM((3, 2, 512), BF),
            pltpu.VMEM((3, 2, 128), BF),
            pltpu.VMEM((ROWS, 512), BF),
            pltpu.VMEM((2, 2048), BF),
            pltpu.SMEM((8,), F32),
            pltpu.SMEM((8,), F32),
            pltpu.SMEM((8,), F32),
            pltpu.SMEM((2,), jnp.int32),
            pltpu.VMEM((ROWS, 1, 512), F32),
            pltpu.VMEM((NR, 1, 128), F32),
            pltpu.VMEM((NR, 2, 128), F32),
            pltpu.VMEM((NR, 2, 128), F32),
            pltpu.VMEM((NR, 2, 1152), F32),
            pltpu.VMEM((NR, 2, 1152), F32),
            pltpu.VMEM((NH, 2, 128), BF),
            pltpu.VMEM((4, 2, 128), F32),
            pltpu.VMEM((NR, 2, 512), BF),
            pltpu.VMEM((ROWS, 1, 512), F32),
            pltpu.VMEM((NH, 1, 512), F32),
            pltpu.VMEM((NR, 1, 128), F32),
            pltpu.VMEM((NH, 1, 512), F32),
            pltpu.VMEM((NH, 1, 128), F32),
            pltpu.VMEM((2, NR, 2, 1024), BF),
            pltpu.VMEM((2, NR, 2, 1024), BF),
            pltpu.VMEM((2, NR, 2, 1024), BF),
            pltpu.VMEM((2, NR, 2, 1024), BF),
            pltpu.VMEM((2, ROWS, 1024), F32),
            pltpu.VMEM((NH, 2, 128), F32),
            pltpu.VMEM((NH, 2, 128), F32),
            pltpu.SemaphoreType.DMA((len(SMALL),)),
            pltpu.SemaphoreType.DMA((4,)),
            pltpu.SemaphoreType.DMA((5,)),
            pltpu.SemaphoreType.DMA((16,)),
            pltpu.SemaphoreType.DMA((16,)),
        ],
        compiler_params=pltpu.CompilerParams(
            collective_id=0, has_side_effects=True, vmem_limit_bytes=56 << 20
        ),
    )(
        hidden,
        norm_gain,
        input_weight,
        group_weight,
        step_weight.T,
        conv_inner_weight,
        conv_group_weight,
        jnp.transpose(conv_inner_state, (1, 0, 2)),
        jnp.transpose(conv_group_state, (1, 0, 2)),
        timestep_bias,
        decay_log,
        skip_gain,
        recurrent_state,
        mixer_gain,
        output_weight,
        final_gain,
        lexicon_matrix,
        token_mask,
        min_share,
    )
    state, inner, group, out, probs = pl.pallas_call(
        finish,
        out_shape=shapes,
        in_specs=[pl.BlockSpec(memory_space=pltpu.VMEM)] * 5,
        out_specs=[hbm] * 5,
        scratch_shapes=[pltpu.SemaphoreType.DMA((5,))],
        compiler_params=pltpu.CompilerParams(vmem_limit_bytes=1 << 20),
    )(*results)
    return (
        state,
        jnp.transpose(inner, (1, 0, 2)),
        jnp.transpose(group, (1, 0, 2)),
        out,
        probs,
    )


def solution(mesh):
    in_specs = (
        P(None, "row"),
        P("row"),
        P("row", None, "head"),
        P("row", "head"),
        P("row", "head"),
        P(None, "head"),
        P(None, "head"),
        P("row", None, "head"),
        P("row", None, "head"),
        P("head"),
        P("head"),
        P("head"),
        P("row", "head", None, None),
        P("head"),
        P("head", "row"),
        P("row"),
        P("row", "head"),
        P("row", "head"),
        P("row"),
    )
    out_specs = (
        P("row", "head", None, None),
        P("row", None, "head"),
        P("row", None, "head"),
        P(None, "row"),
        P("row", "head"),
    )
    return jax.shard_map(local, mesh=mesh, in_specs=in_specs, out_specs=out_specs, check_vma=False)
```

```python
import jax
import jax.numpy as jnp
from jax import lax
from jax.experimental import pallas as pl
from jax.experimental.pallas import tpu as pltpu
from jax.sharding import PartitionSpec as P

D = 8192
HEADS = 256
HEAD_DIM = 64
STATE = 256
GROUPS = 8
NR = 16
NH = 32
ROWS = 32
EPSILON = 1e-05
INVERSE_HEAT = 1.25
FIXED_POINT = 65536.0
NEG_LARGE = -1e30
MESH = pl.DeviceIdType.MESH
BF = jnp.bfloat16
F32 = jnp.float32


def silu(v):
    return v / (1.0 + jnp.exp(-v))


def iota(shape, axis):
    return lax.broadcasted_iota(jnp.int32, shape, axis)


def dot(a, b):
    return jnp.dot(a, b, preferred_element_type=F32)


def dot_nt(a, b):
    return lax.dot_general(a, b, (((1,), (1,)), ((), ())), preferred_element_type=F32)


N_IN = 19
SMALL = (
    "hidden",
    "norm_gain",
    "group_weight",
    "step_weight",
    "conv_inner_weight",
    "conv_group_weight",
    "conv_inner_state",
    "conv_group_state",
    "mixer_gain",
    "final_gain",
    "token_mask",
    "recurrent_state",
    "output_weight",
    "lexicon_matrix",
    "timestep_bias",
    "decay_log",
    "skip_gain",
    "min_share",
)


def kernel(
    hidden_h,
    norm_gain_h,
    input_weight_h,
    group_weight_h,
    step_weight_h,
    conv_inner_weight_h,
    conv_group_weight_h,
    conv_inner_state_h,
    conv_group_state_h,
    timestep_bias_h,
    decay_log_h,
    skip_gain_h,
    recurrent_state_h,
    mixer_gain_h,
    output_weight_h,
    final_gain_h,
    lexicon_h,
    token_mask_h,
    min_share_h,
    next_state_h,
    next_conv_inner_h,
    next_conv_group_h,
    layer_out_h,
    next_probs_h,
    hidden_v,
    norm_gain_v,
    input_weight_v,
    group_weight_v,
    step_weight_v,
    conv_inner_weight_v,
    conv_group_weight_v,
    conv_inner_state_v,
    conv_group_state_v,
    recurrent_state_v,
    mixer_gain_v,
    output_weight_v,
    final_gain_v,
    lexicon_v,
    token_mask_v,
    next_state_v,
    next_conv_inner,
    next_conv_group,
    layer_out,
    next_probs,
    timestep_bias,
    decay_log,
    skip_gain,
    min_share,
    state_turned,
    hidden_rows,
    square_buf,
    group_part,
    group_buf,
    in_part,
    in_buf,
    pair_buf,
    share_mine,
    share_buf,
    mixer_buf,
    mixed_part,
    mixed_buf,
    scale_buf,
    out_buf,
    norm_buf,
    logit_part,
    logit_buf,
    rest_part,
    rest_buf,
    lexicon_lent,
    exact_mine,
    exact_lent,
    peak_buf,
    total_buf,
    in_sem,
    weight_sem,
    save_sem,
    send_sem,
    recv_sem,
):
    i = lax.axis_index("row")
    j = lax.axis_index("head")

    barrier = pltpu.get_barrier_semaphore()

    def far_first(k, n):
        return n // 2 + (2 * (k % 2) - 1) * ((k + 1) // 2)

    def greet_row(k, carry):
        to = lax.rem(i + far_first(k, NR), NR)
        pl.semaphore_signal(barrier, inc=1, device_id=(to, j), device_id_type=MESH)
        return carry

    def greet_head(k, carry):
        to = lax.rem(j + far_first(k, NH), NH)
        pl.semaphore_signal(barrier, inc=1, device_id=(i, to), device_id_type=MESH)
        return carry

    lax.fori_loop(0, NR - 1, greet_row, 0)
    lax.fori_loop(0, NH - 1, greet_head, 0)

    loads = {
        "hidden": (hidden_h, hidden_v),
        "norm_gain": (norm_gain_h, norm_gain_v),
        "group_weight": (group_weight_h, group_weight_v),
        "step_weight": (step_weight_h, step_weight_v),
        "conv_inner_weight": (conv_inner_weight_h, conv_inner_weight_v),
        "conv_group_weight": (conv_group_weight_h, conv_group_weight_v),
        "conv_inner_state": (conv_inner_state_h, conv_inner_state_v),
        "conv_group_state": (conv_group_state_h, conv_group_state_v),
        "mixer_gain": (mixer_gain_h, mixer_gain_v),
        "final_gain": (final_gain_h, final_gain_v),
        "token_mask": (token_mask_h, token_mask_v),
        "recurrent_state": (recurrent_state_h, recurrent_state_v),
        "output_weight": (output_weight_h, output_weight_v),
        "lexicon_matrix": (
            lexicon_h.at[:, pl.ds(pl.multiple_of((i % 2) * 1024, 1024), 1024)],
            lexicon_v,
        ),
        "timestep_bias": (timestep_bias_h, timestep_bias),
        "decay_log": (decay_log_h, decay_log),
        "skip_gain": (skip_gain_h, skip_gain),
        "min_share": (min_share_h, min_share),
    }

    def load(name):
        src, dst = loads[name]
        return pltpu.make_async_copy(src, dst, in_sem.at[SMALL.index(name)])

    def load_weight(block):
        return pltpu.make_async_copy(
            input_weight_h.at[:, :, pl.ds(block * 128, 128)],
            input_weight_v.at[block],
            weight_sem.at[block],
        )

    load("hidden").start()
    load("norm_gain").start()
    for block in range(4):
        load_weight(block).start()
    for name in SMALL[2:]:
        load(name).start()

    def send_row(phase, src, dst):
        def step(k, carry):
            to = lax.rem(i + far_first(k, NR), NR)
            pltpu.make_async_remote_copy(
                src_ref=dst.at[i] if src is None else src.at[to],
                dst_ref=dst.at[i],
                send_sem=send_sem.at[phase],
                recv_sem=recv_sem.at[phase],
                device_id=(to, j),
                device_id_type=MESH,
            ).start()
            return carry

        lax.fori_loop(0, NR - 1, step, 0)

    def send_head(phase, src, dst):
        def step(k, carry):
            to = lax.rem(j + far_first(k, NH), NH)
            pltpu.make_async_remote_copy(
                src_ref=dst.at[j] if src is None else src.at[to],
                dst_ref=dst.at[j],
                send_sem=send_sem.at[phase],
                recv_sem=recv_sem.at[phase],
                device_id=(i, to),
                device_id_type=MESH,
            ).start()
            return carry

        lax.fori_loop(0, NH - 1, step, 0)

    def arrived(phase, dst):
        rest = dst.at[pl.ds(0, dst.shape[0] - 1)]
        pltpu.make_async_copy(rest, rest, recv_sem.at[phase]).wait()

    def sent(phase, dst):
        rest = dst.at[pl.ds(0, dst.shape[0] - 1)]
        pltpu.make_async_copy(rest, rest, send_sem.at[phase]).wait()

    sibling = i + 1 - 2 * (i % 2)
    half_slot = (i % 2) * 8 + i // 2

    def to_sibling(phase, src, dst):
        return pltpu.make_async_remote_copy(
            src_ref=src,
            dst_ref=dst,
            send_sem=send_sem.at[phase],
            recv_sem=recv_sem.at[phase],
            device_id=(sibling, j),
            device_id_type=MESH,
        )

    lend_lexicon = to_sibling(
        14,
        lexicon_h.at[:, pl.ds(pl.multiple_of((1 - i % 2) * 1024, 1024), 1024)],
        lexicon_lent,
    )

    def send_half(phase, src, dst):
        def step(k, carry):
            to = lax.rem(i + far_first(k, NR), NR)
            pltpu.make_async_remote_copy(
                src_ref=src.at[to],
                dst_ref=dst.at[half_slot],
                send_sem=send_sem.at[phase],
                recv_sem=recv_sem.at[phase],
                device_id=(to, j),
                device_id_type=MESH,
            ).start()
            return carry

        lax.fori_loop(0, NR - 1, step, 0)

    column = (j % 4) * NR

    def send_across(phase, src, dst):
        def step(k, carry):
            to = (lax.rem(i + 8 + k // 3, NR), j - j % 4 + lax.rem(j + 1 + k % 3, 4))
            pltpu.make_async_remote_copy(
                src_ref=src,
                dst_ref=dst.at[column + i],
                send_sem=send_sem.at[phase],
                recv_sem=recv_sem.at[phase],
                device_id=to,
                device_id_type=MESH,
            ).start()
            return carry

        lax.fori_loop(0, 3 * NR, step, 0)

    def save(at, src, dst):
        copy = pltpu.make_async_copy(src, dst, save_sem.at[at])
        copy.start()
        return copy

    share_buf[pl.ds(column, NR)] = jnp.zeros((NR, 2, 128), F32)
    load("hidden").wait()
    load("norm_gain").wait()
    hidden_wide = hidden_v[...].astype(F32)
    hidden_rows[:, 0, :] = hidden_wide
    squares = jnp.sum(hidden_wide * hidden_wide, axis=1, keepdims=True)
    diagonal = iota((ROWS, 128), 0) == iota((ROWS, 128), 1)
    square_buf[i] = jnp.sum(jnp.where(diagonal, squares, 0.0), axis=0, keepdims=True)
    depth_at, slot_at = iota((128, 256), 0), iota((128, 256), 1)
    spread_even = (slot_at == 2 * depth_at).astype(F32).astype(BF)
    spread_odd = (slot_at == 2 * depth_at + 1).astype(F32).astype(BF)
    load("group_weight").wait()
    pl.semaphore_wait(barrier, NR + NH - 2)
    send_row(8, None, square_buf)
    load("recurrent_state").wait()
    for r in range(2):
        state_turned[r] = recurrent_state_v[r].reshape(512, 256).T
    arrived(8, square_buf)
    square_total = jnp.sum(square_buf[...], axis=0)
    row_total = jnp.sum(jnp.where(diagonal, square_total, 0.0), axis=1, keepdims=True)
    hidden_scale = lax.rsqrt(row_total / D + EPSILON)

    gained = (hidden_wide * hidden_scale * norm_gain_v[...].astype(F32).reshape(1, 512)).astype(BF)
    group_part[...] = dot(gained, group_weight_v[...]).reshape(NR, 2, 128)
    send_row(0, group_part, group_buf)
    group_buf[i] = group_part[i]
    blocks = [gained[:, 128 * b : 128 * b + 128] for b in range(4)]
    doubled = jnp.concatenate(
        [
            jnp.concatenate([dot(part, spread_even) for part in blocks], axis=1),
            jnp.concatenate([dot(part, spread_odd) for part in blocks], axis=1),
        ],
        axis=0,
    ).astype(BF)
    for block in range(4):
        load_weight(block).wait()
        both = dot(doubled, input_weight_v[block].reshape(1024, 128))
        in_part[:, :, 128 * block : 128 * block + 128] = both[:32].reshape(NR, 2, 128)
        in_part[:, :, 512 + 128 * block : 640 + 128 * block] = both[32:].reshape(NR, 2, 128)
    load("step_weight").wait()
    step_rows = jnp.concatenate(
        [step_weight_v[...].astype(F32), jnp.zeros((120, 512), F32)], axis=0
    ).astype(BF)
    in_part[:, :, 1024:1152] = dot_nt(gained, step_rows).reshape(NR, 2, 128)
    send_row(11, in_part, in_buf)
    in_buf[i] = in_part[i]

    for name in ("conv_inner_weight", "conv_group_weight", "conv_inner_state", "conv_group_state"):
        load(name).wait()
    arrived(0, group_buf)
    group_new = jnp.sum(group_buf[...], axis=0).astype(BF)
    group_old = conv_group_state_v[...].astype(F32)
    group_taps = conv_group_weight_v[...].astype(F32)
    group_mix = (
        group_old[0] * group_taps[0:1]
        + group_old[1] * group_taps[1:2]
        + group_old[2] * group_taps[2:3]
        + group_new.astype(F32) * group_taps[3:4]
    )
    pair_buf[j] = silu(group_mix).astype(BF)
    send_head(1, None, pair_buf)
    lend_lexicon.start()

    next_conv_group[0] = conv_group_state_v[1]
    next_conv_group[1] = conv_group_state_v[2]
    next_conv_group[2] = group_new
    arrived(11, in_buf)
    projected = jnp.sum(in_buf[...], axis=0)
    inner_new = projected[:, 512:1024].astype(BF)
    next_conv_inner[0] = conv_inner_state_v[1]
    next_conv_inner[1] = conv_inner_state_v[2]
    next_conv_inner[2] = inner_new
    inner_old = conv_inner_state_v[...].astype(F32)
    inner_taps = conv_inner_weight_v[...].astype(F32)
    conv_inner = silu(
        inner_old[0] * inner_taps[0:1]
        + inner_old[1] * inner_taps[1:2]
        + inner_old[2] * inner_taps[2:3]
        + inner_new.astype(F32) * inner_taps[3:4]
    )
    gate = silu(projected[:, :512])
    step_raw = projected[:, 1024:1032]
    saves = [
        save(1, next_conv_inner, next_conv_inner_h),
        save(2, next_conv_group, next_conv_group_h),
    ]
    for name in ("timestep_bias", "decay_log", "skip_gain"):
        load(name).wait()
    head_of = iota((2, 512), 1) // HEAD_DIM
    step_in = jnp.zeros((2, 512), F32)
    rate_log = jnp.zeros((2, 512), F32)
    skip = jnp.zeros((2, 512), F32)
    for h in range(8):
        here = head_of == h
        step_in = jnp.where(here, step_raw[:, h : h + 1] + timestep_bias[h], step_in)
        rate_log = jnp.where(here, decay_log[h], rate_log)
        skip = jnp.where(here, skip_gain[h], skip)
    step_size = jnp.maximum(step_in, 0.0) + jnp.log1p(jnp.exp(-jnp.abs(step_in)))
    decay = jnp.exp(-step_size * jnp.exp(rate_log))
    driven = step_size * conv_inner

    group_at = j // (NH // GROUPS)
    channel_at, entry_at = iota((128, 256), 0), iota((128, 256), 1)
    pick = (channel_at == (entry_at % 16) * GROUPS + group_at).astype(F32).astype(BF)
    source_at, entry_of = iota((NH, 256), 0), iota((NH, 256), 1) // 16
    load("mixer_gain").wait()
    arrived(1, pair_buf)
    inputs, readouts = [], []
    for r in range(2):
        picked = dot(pair_buf[:, r, :], pick)
        inputs.append(
            jnp.sum(jnp.where(source_at == entry_of, picked, 0.0), axis=0, keepdims=True)
        )
        readouts.append(
            jnp.sum(jnp.where(source_at == entry_of + 16, picked, 0.0), axis=0, keepdims=True)
        )
    readout = []
    for r in range(2):
        old_read = dot(readouts[r].astype(BF), state_turned[r])
        pair_dot = jnp.sum(inputs[r] * readouts[r], axis=1, keepdims=True)
        readout.append(
            decay[r : r + 1] * old_read
            + driven[r : r + 1] * pair_dot
            + skip[r : r + 1] * conv_inner[r : r + 1]
        )
    gated = jnp.concatenate(readout, axis=0) * gate
    gated_squares = jnp.sum(gated * gated, axis=1, keepdims=True)
    mixer_gain_wide = mixer_gain_v[...].astype(F32).reshape(1, 512)
    mixer_buf[i, :, 0:512] = gated
    mixer_buf[i, :, 512:640] = jnp.broadcast_to(gated_squares, (2, 128))
    share_mine[...] = jnp.broadcast_to(gated_squares, (2, 128))
    send_row(2, None, mixer_buf)
    send_across(9, share_mine, share_buf)

    rows8 = jnp.concatenate([driven, decay, jnp.zeros((4, 512), F32)], axis=0)
    columns = rows8.T
    for r in range(2):
        for h in range(8):
            at = slice(64 * h, 64 * h + 64)
            fresh = (
                columns[at, 2 + r : 3 + r] * recurrent_state_v[r, h].astype(F32)
                + columns[at, r : r + 1] * inputs[r]
            )
            next_state_v[r, h] = fresh.astype(BF)
    saves.append(save(0, next_state_v, next_state_h))

    load("output_weight").wait()
    arrived(2, mixer_buf)
    rest = share_buf.at[pl.ds(0, 3 * NR)]
    pltpu.make_async_copy(rest, rest, recv_sem.at[9]).wait()
    group_total = mixer_buf[:, :, 512:640]
    for at in range(4):
        group_total += share_buf[NR * at : NR * at + NR]
    group_scale = lax.rsqrt(group_total / (HEADS * HEAD_DIM // GROUPS) + EPSILON)[:, :, 0:1]
    mixer_rows = (mixer_buf[:, :, 0:512] * group_scale * mixer_gain_wide).astype(BF)
    mixer_rows = mixer_rows.reshape(ROWS, 512)
    mixed_part[:, 0, :] = dot(mixer_rows, output_weight_v[...])
    send_head(3, mixed_part, mixed_buf)
    mixed_buf[j] = mixed_part[j]

    load("final_gain").wait()
    final_gain_wide = final_gain_v[...].astype(F32).reshape(1, 512)
    arrived(3, mixed_buf)
    mixed = jnp.sum(mixed_buf[...], axis=0)
    out_mine = (hidden_rows[j] + mixed).astype(BF).astype(F32)
    scale_buf[i] = jnp.broadcast_to(jnp.sum(out_mine * out_mine, axis=1, keepdims=True), (1, 128))
    send_row(10, None, scale_buf)
    out_buf[j] = out_mine
    send_head(4, None, out_buf)
    arrived(10, scale_buf)
    norm_buf[j] = lax.rsqrt(jnp.sum(scale_buf[...], axis=0) / D + EPSILON)
    send_head(5, None, norm_buf)

    load("lexicon_matrix").wait()
    load("token_mask").wait()
    load("min_share").wait()
    arrived(4, out_buf)
    out_wide = out_buf[:, 0, :]
    scaled = out_wide * final_gain_wide
    upper = scaled.astype(BF)
    lower = (scaled - upper.astype(F32)).astype(BF)
    exact_mine[0:ROWS] = upper
    exact_mine[ROWS:] = lower
    lend_rows = to_sibling(15, exact_mine, exact_lent)
    lend_rows.start()
    both = dot(exact_mine[...], lexicon_v[...])
    lend_lexicon.wait()
    lend_rows.wait()
    both += dot(exact_lent[...], lexicon_lent[...])
    main = both[:ROWS] + both[ROWS:]
    coarse = main.astype(BF)
    logit_part[...] = coarse.reshape(NR, 2, 1024)
    send_half(12, logit_part, logit_buf)
    logit_buf[half_slot] = logit_part[i]
    main_rest = main - coarse.astype(F32)
    scaled_lent = exact_lent[0:ROWS].astype(F32) + exact_lent[ROWS:].astype(F32)
    layer_out[...] = out_wide.astype(BF)
    saves.append(save(3, layer_out, layer_out_h))

    arrived(5, norm_buf)
    row_scale = norm_buf[:, 0, :][:, 0:1]

    def rounding(product):
        exact = product * row_scale
        return (exact.astype(BF).astype(F32) - exact).astype(BF)

    rest = dot(rounding(scaled), lexicon_v[...]) + dot(rounding(scaled_lent), lexicon_lent[...])
    rest_part[...] = (rest + main_rest * row_scale).astype(BF).reshape(NR, 2, 1024)
    send_half(13, rest_part, rest_buf)
    rest_buf[half_slot] = rest_part[i]
    scale_mine = jnp.concatenate([norm_buf[2 * i], norm_buf[2 * i + 1]], axis=0)[:, 0:1]

    allowed = token_mask_v[...] > 0
    row_at = iota((2, 1), 0)
    floor_share = (
        jnp.where(row_at == 0, min_share[0], min_share[1]).astype(F32) / FIXED_POINT
    )

    def half_sums(buf):
        return jnp.concatenate(
            [
                jnp.sum(buf[0:8].astype(F32), axis=0),
                jnp.sum(buf[8:16].astype(F32), axis=0),
            ],
            axis=1,
        )

    arrived(12, logit_buf)
    main_sum = half_sums(logit_buf) * scale_mine
    arrived(13, rest_buf)
    scores = (main_sum + half_sums(rest_buf)) * INVERSE_HEAT
    peak_mine = jnp.max(jnp.where(allowed, scores, NEG_LARGE), axis=1, keepdims=True)
    peak_buf[j] = jnp.broadcast_to(peak_mine, (2, 128))
    send_head(6, None, peak_buf)
    arrived(6, peak_buf)
    peak = jnp.max(peak_buf[...], axis=0)[:, 0:1]
    ratio = jnp.where(allowed, jnp.exp(scores - peak), 0.0)
    weights = ratio * jnp.clip(ratio / floor_share - 1.0, 0.0, 1.0)
    total_mine = jnp.sum(weights, axis=1, keepdims=True)
    total_buf[j] = jnp.broadcast_to(total_mine, (2, 128))
    send_head(7, None, total_buf)
    arrived(7, total_buf)
    total = jnp.sum(total_buf[...], axis=0)[:, 0:1]
    next_probs[...] = (weights / total).astype(BF)

    saves.append(save(4, next_probs, next_probs_h))
    for copy in saves:
        copy.wait()
    for phase, dst in enumerate(
        (
            group_buf,
            pair_buf,
            mixer_buf,
            mixed_buf,
            out_buf,
            norm_buf,
            peak_buf,
            total_buf,
            square_buf,
            share_buf.at[pl.ds(0, 3 * NR + 1)],
            scale_buf,
            in_buf,
            logit_buf,
            rest_buf,
        )
    ):
        sent(phase, dst)


def finish(*refs):
    sems = refs[-1]
    copies = [
        pltpu.make_async_copy(refs[at], refs[at + 5], sems.at[at]) for at in range(5)
    ]
    for copy in copies:
        copy.start()
    for copy in copies:
        copy.wait()


def local(
    hidden,
    norm_gain,
    input_weight,
    group_weight,
    step_weight,
    conv_inner_weight,
    conv_group_weight,
    conv_inner_state,
    conv_group_state,
    timestep_bias,
    decay_log,
    skip_gain,
    recurrent_state,
    mixer_gain,
    output_weight,
    final_gain,
    lexicon_matrix,
    token_mask,
    min_share,
):
    hbm = pl.BlockSpec(memory_space=pltpu.HBM)
    in_specs = [hbm] * N_IN
    shapes = (
            jax.ShapeDtypeStruct((2, 8, 64, 256), BF),
            jax.ShapeDtypeStruct((3, 2, 512), BF),
            jax.ShapeDtypeStruct((3, 2, 128), BF),
            jax.ShapeDtypeStruct((ROWS, 512), BF),
            jax.ShapeDtypeStruct((2, 2048), BF),
    )
    results = pl.pallas_call(
        kernel,
        out_shape=tuple(pltpu.VMEM(shape.shape, BF) for shape in shapes),
        in_specs=in_specs,
        out_specs=(pl.BlockSpec(memory_space=pltpu.VMEM),) * 5,
        scratch_shapes=[
            pltpu.VMEM((ROWS, 512), BF),
            pltpu.VMEM((512,), BF),
            pltpu.VMEM((4, 512, 2, 128), BF),
            pltpu.VMEM((512, 128), BF),
            pltpu.VMEM((8, 512), BF),
            pltpu.VMEM((4, 512), BF),
            pltpu.VMEM((4, 128), BF),
            pltpu.VMEM((3, 2, 512), BF),
            pltpu.VMEM((3, 2, 128), BF),
            pltpu.VMEM((2, 8, 64, 256), BF),
            pltpu.VMEM((512,), BF),
            pltpu.VMEM((512, 512), BF),
            pltpu.VMEM((512,), BF),
            pltpu.VMEM((512, 1024), BF),
            pltpu.VMEM((2, 2048), jnp.int32),
            pltpu.VMEM((2, 8, 64, 256), BF),
            pltpu.VMEM((3, 2, 512), BF),
            pltpu.VMEM((3, 2, 128), BF),
            pltpu.VMEM((ROWS, 512), BF),
            pltpu.VMEM((2, 2048), BF),
            pltpu.SMEM((8,), F32),
            pltpu.SMEM((8,), F32),
            pltpu.SMEM((8,), F32),
            pltpu.SMEM((2,), jnp.int32),
            pltpu.VMEM((2, 256, 512), BF),
            pltpu.VMEM((ROWS, 1, 512), F32),
            pltpu.VMEM((NR, 1, 128), F32),
            pltpu.VMEM((NR, 2, 128), F32),
            pltpu.VMEM((NR, 2, 128), F32),
            pltpu.VMEM((NR, 2, 1152), F32),
            pltpu.VMEM((NR, 2, 1152), F32),
            pltpu.VMEM((NH, 2, 128), BF),
            pltpu.VMEM((2, 128), F32),
            pltpu.VMEM((4 * NR, 2, 128), F32),
            pltpu.VMEM((NR, 2, 640), F32),
            pltpu.VMEM((ROWS, 1, 512), F32),
            pltpu.VMEM((NH, 1, 512), F32),
            pltpu.VMEM((NR, 1, 128), F32),
            pltpu.VMEM((NH, 1, 512), F32),
            pltpu.VMEM((NH, 1, 128), F32),
            pltpu.VMEM((NR, 2, 1024), BF),
            pltpu.VMEM((NR, 2, 1024), BF),
            pltpu.VMEM((NR, 2, 1024), BF),
            pltpu.VMEM((NR, 2, 1024), BF),
            pltpu.VMEM((512, 1024), BF),
            pltpu.VMEM((2 * ROWS, 512), BF),
            pltpu.VMEM((2 * ROWS, 512), BF),
            pltpu.VMEM((NH, 2, 128), F32),
            pltpu.VMEM((NH, 2, 128), F32),
            pltpu.SemaphoreType.DMA((len(SMALL),)),
            pltpu.SemaphoreType.DMA((4,)),
            pltpu.SemaphoreType.DMA((5,)),
            pltpu.SemaphoreType.DMA((16,)),
            pltpu.SemaphoreType.DMA((16,)),
        ],
        compiler_params=pltpu.CompilerParams(
            collective_id=0, has_side_effects=True, vmem_limit_bytes=56 << 20
        ),
    )(
        hidden,
        norm_gain,
        input_weight,
        group_weight,
        step_weight.T,
        conv_inner_weight,
        conv_group_weight,
        jnp.transpose(conv_inner_state, (1, 0, 2)),
        jnp.transpose(conv_group_state, (1, 0, 2)),
        timestep_bias,
        decay_log,
        skip_gain,
        recurrent_state,
        mixer_gain,
        output_weight,
        final_gain,
        lexicon_matrix,
        token_mask,
        min_share,
    )
    state, inner, group, out, probs = pl.pallas_call(
        finish,
        out_shape=shapes,
        in_specs=[pl.BlockSpec(memory_space=pltpu.VMEM)] * 5,
        out_specs=[hbm] * 5,
        scratch_shapes=[pltpu.SemaphoreType.DMA((5,))],
        compiler_params=pltpu.CompilerParams(vmem_limit_bytes=1 << 20),
    )(*results)
    return (
        state,
        jnp.transpose(inner, (1, 0, 2)),
        jnp.transpose(group, (1, 0, 2)),
        out,
        probs,
    )


def solution(mesh):
    in_specs = (
        P(None, "row"),
        P("row"),
        P("row", None, "head"),
        P("row", "head"),
        P("row", "head"),
        P(None, "head"),
        P(None, "head"),
        P("row", None, "head"),
        P("row", None, "head"),
        P("head"),
        P("head"),
        P("head"),
        P("row", "head", None, None),
        P("head"),
        P("head", "row"),
        P("row"),
        P("row", "head"),
        P("row", "head"),
        P("row"),
    )
    out_specs = (
        P("row", "head", None, None),
        P("row", None, "head"),
        P("row", None, "head"),
        P(None, "row"),
        P("row", "head"),
    )
    return jax.shard_map(local, mesh=mesh, in_specs=in_specs, out_specs=out_specs, check_vma=False)
```

```python
import jax
import jax.numpy as jnp
from jax import lax
from jax.experimental import pallas as pl
from jax.experimental.pallas import tpu as pltpu
from jax.sharding import PartitionSpec as P

D = 8192
HEADS = 256
HEAD_DIM = 64
STATE = 256
GROUPS = 8
NR = 16
NH = 32
ROWS = 32
EPSILON = 1e-05
INVERSE_HEAT = 1.25
FIXED_POINT = 65536.0
NEG_LARGE = -1e30
MESH = pl.DeviceIdType.MESH
BF = jnp.bfloat16
F32 = jnp.float32


def silu(v):
    return v / (1.0 + jnp.exp(-v))


def iota(shape, axis):
    return lax.broadcasted_iota(jnp.int32, shape, axis)


def dot(a, b):
    return jnp.dot(a, b, preferred_element_type=F32)


def dot_nt(a, b):
    return lax.dot_general(a, b, (((1,), (1,)), ((), ())), preferred_element_type=F32)


N_IN = 19
SMALL = (
    "hidden",
    "norm_gain",
    "group_weight",
    "step_weight",
    "conv_inner_weight",
    "conv_group_weight",
    "conv_inner_state",
    "conv_group_state",
    "mixer_gain",
    "final_gain",
    "token_mask",
    "recurrent_state",
    "output_weight",
    "lexicon_matrix",
    "timestep_bias",
    "decay_log",
    "skip_gain",
    "min_share",
)


def kernel(
    hidden_h,
    norm_gain_h,
    input_weight_h,
    group_weight_h,
    step_weight_h,
    conv_inner_weight_h,
    conv_group_weight_h,
    conv_inner_state_h,
    conv_group_state_h,
    timestep_bias_h,
    decay_log_h,
    skip_gain_h,
    recurrent_state_h,
    mixer_gain_h,
    output_weight_h,
    final_gain_h,
    lexicon_h,
    token_mask_h,
    min_share_h,
    next_state_h,
    next_conv_inner_h,
    next_conv_group_h,
    layer_out_h,
    next_probs_h,
    hidden_v,
    norm_gain_v,
    input_weight_v,
    group_weight_v,
    step_weight_v,
    conv_inner_weight_v,
    conv_group_weight_v,
    conv_inner_state_v,
    conv_group_state_v,
    recurrent_state_v,
    mixer_gain_v,
    output_weight_v,
    final_gain_v,
    lexicon_v,
    token_mask_v,
    next_state_v,
    next_conv_inner,
    next_conv_group,
    layer_out,
    next_probs,
    timestep_bias,
    decay_log,
    skip_gain,
    min_share,
    state_turned,
    hidden_rows,
    square_buf,
    group_part,
    group_buf,
    in_part,
    in_buf,
    pair_buf,
    share_mine,
    share_buf,
    mixer_buf,
    mixed_part,
    mixed_buf,
    scale_buf,
    out_buf,
    norm_buf,
    logit_part,
    logit_buf,
    rest_part,
    rest_buf,
    lexicon_lent,
    exact_mine,
    exact_lent,
    peak_buf,
    total_buf,
    in_sem,
    weight_sem,
    save_sem,
    send_sem,
    recv_sem,
    column_sem,
):
    i = lax.axis_index("row")
    j = lax.axis_index("head")

    barrier = pltpu.get_barrier_semaphore()

    def far_first(k, n):
        return n // 2 + (2 * (k % 2) - 1) * ((k + 1) // 2)

    def greet_row(k, carry):
        to = lax.rem(i + far_first(k, NR), NR)
        pl.semaphore_signal(barrier, inc=1, device_id=(to, j), device_id_type=MESH)
        return carry

    lax.fori_loop(0, NR - 1, greet_row, 0)
    offsets = (1 + i, 17 + i - i // 15)
    for offset in offsets:
        to = lax.rem(j + offset, NH)
        pl.semaphore_signal(barrier, inc=1, device_id=(i, to), device_id_type=MESH)

    loads = {
        "hidden": (hidden_h, hidden_v),
        "norm_gain": (norm_gain_h, norm_gain_v),
        "group_weight": (group_weight_h, group_weight_v),
        "step_weight": (step_weight_h, step_weight_v),
        "conv_inner_weight": (conv_inner_weight_h, conv_inner_weight_v),
        "conv_group_weight": (conv_group_weight_h, conv_group_weight_v),
        "conv_inner_state": (conv_inner_state_h, conv_inner_state_v),
        "conv_group_state": (conv_group_state_h, conv_group_state_v),
        "mixer_gain": (mixer_gain_h, mixer_gain_v),
        "final_gain": (final_gain_h, final_gain_v),
        "token_mask": (token_mask_h, token_mask_v),
        "recurrent_state": (recurrent_state_h, recurrent_state_v),
        "output_weight": (output_weight_h, output_weight_v),
        "lexicon_matrix": (
            lexicon_h.at[:, pl.ds(pl.multiple_of((i % 2) * 1024, 1024), 1024)],
            lexicon_v,
        ),
        "timestep_bias": (timestep_bias_h, timestep_bias),
        "decay_log": (decay_log_h, decay_log),
        "skip_gain": (skip_gain_h, skip_gain),
        "min_share": (min_share_h, min_share),
    }

    def load(name):
        src, dst = loads[name]
        return pltpu.make_async_copy(src, dst, in_sem.at[SMALL.index(name)])

    def load_weight(block):
        return pltpu.make_async_copy(
            input_weight_h.at[:, :, pl.ds(block * 128, 128)],
            input_weight_v.at[block],
            weight_sem.at[block],
        )

    load("hidden").start()
    load("norm_gain").start()
    for block in range(4):
        load_weight(block).start()
    for name in SMALL[2:]:
        load(name).start()

    def send_row(phase, src, dst):
        def step(k, carry):
            to = lax.rem(i + far_first(k, NR), NR)
            pltpu.make_async_remote_copy(
                src_ref=dst.at[i] if src is None else src.at[to],
                dst_ref=dst.at[i],
                send_sem=send_sem.at[phase],
                recv_sem=recv_sem.at[phase],
                device_id=(to, j),
                device_id_type=MESH,
            ).start()
            return carry

        lax.fori_loop(0, NR - 1, step, 0)

    def send_head(phase, src, dst):
        def step(k, carry):
            to = lax.rem(j + far_first(k, NH), NH)
            pltpu.make_async_remote_copy(
                src_ref=dst.at[j] if src is None else src.at[to],
                dst_ref=dst.at[j],
                send_sem=send_sem.at[phase],
                recv_sem=recv_sem.at[phase],
                device_id=(i, to),
                device_id_type=MESH,
            ).start()
            return carry

        lax.fori_loop(0, NH - 1, step, 0)

    def arrived(phase, dst):
        rest = dst.at[pl.ds(0, dst.shape[0] - 1)]
        pltpu.make_async_copy(rest, rest, recv_sem.at[phase]).wait()

    def sent(phase, dst):
        rest = dst.at[pl.ds(0, dst.shape[0] - 1)]
        pltpu.make_async_copy(rest, rest, send_sem.at[phase]).wait()

    sibling = i + 1 - 2 * (i % 2)
    half_slot = (i % 2) * 8 + i // 2

    def to_sibling(phase, src, dst):
        return pltpu.make_async_remote_copy(
            src_ref=src,
            dst_ref=dst,
            send_sem=send_sem.at[phase],
            recv_sem=recv_sem.at[phase],
            device_id=(sibling, j),
            device_id_type=MESH,
        )

    lend_lexicon = to_sibling(
        14,
        lexicon_h.at[:, pl.ds(pl.multiple_of((1 - i % 2) * 1024, 1024), 1024)],
        lexicon_lent,
    )

    def send_half(phase, src, dst):
        def step(k, carry):
            to = lax.rem(i + far_first(k, NR), NR)
            pltpu.make_async_remote_copy(
                src_ref=src.at[to],
                dst_ref=dst.at[half_slot],
                send_sem=send_sem.at[phase],
                recv_sem=recv_sem.at[phase],
                device_id=(to, j),
                device_id_type=MESH,
            ).start()
            return carry

        lax.fori_loop(0, NR - 1, step, 0)

    column = (j % 4) * NR

    def send_across(phase, src, dst):
        def step(k, carry):
            to = (lax.rem(i + far_first(k // 3, NR), NR), j - j % 4 + lax.rem(j + 1 + k % 3, 4))
            pltpu.make_async_remote_copy(
                src_ref=src,
                dst_ref=dst.at[column + i],
                send_sem=send_sem.at[phase],
                recv_sem=recv_sem.at[phase],
                device_id=to,
                device_id_type=MESH,
            ).start()
            return carry

        lax.fori_loop(0, 3 * NR, step, 0)

    def save(at, src, dst):
        copy = pltpu.make_async_copy(src, dst, save_sem.at[at])
        copy.start()
        return copy

    share_buf[pl.ds(column, NR)] = jnp.zeros((NR, 2, 128), F32)
    load("hidden").wait()
    load("norm_gain").wait()
    hidden_wide = hidden_v[...].astype(F32)
    hidden_rows[:, 0, :] = hidden_wide
    squares = jnp.sum(hidden_wide * hidden_wide, axis=1, keepdims=True)
    diagonal = iota((ROWS, 128), 0) == iota((ROWS, 128), 1)
    square_buf[i] = jnp.sum(jnp.where(diagonal, squares, 0.0), axis=0, keepdims=True)
    depth_at, slot_at = iota((128, 256), 0), iota((128, 256), 1)
    spread_even = (slot_at == 2 * depth_at).astype(F32).astype(BF)
    spread_odd = (slot_at == 2 * depth_at + 1).astype(F32).astype(BF)
    load("group_weight").wait()
    pl.semaphore_wait(barrier, NR + 1)
    send_row(8, None, square_buf)
    for offset in offsets:
        to = lax.rem(j + NH - offset, NH)
        pl.semaphore_signal(column_sem, inc=1, device_id=(i, to), device_id_type=MESH)
    load("recurrent_state").wait()
    for r in range(2):
        state_turned[r] = recurrent_state_v[r].reshape(512, 256).T
    arrived(8, square_buf)
    square_total = jnp.sum(square_buf[...], axis=0)
    row_total = jnp.sum(jnp.where(diagonal, square_total, 0.0), axis=1, keepdims=True)
    hidden_scale = lax.rsqrt(row_total / D + EPSILON)

    gained = (hidden_wide * hidden_scale * norm_gain_v[...].astype(F32).reshape(1, 512)).astype(BF)
    group_part[...] = dot(gained, group_weight_v[...]).reshape(NR, 2, 128)
    pl.semaphore_wait(column_sem, 2)
    send_row(0, group_part, group_buf)
    group_buf[i] = group_part[i]
    blocks = [gained[:, 128 * b : 128 * b + 128] for b in range(4)]
    doubled = jnp.concatenate(
        [
            jnp.concatenate([dot(part, spread_even) for part in blocks], axis=1),
            jnp.concatenate([dot(part, spread_odd) for part in blocks], axis=1),
        ],
        axis=0,
    ).astype(BF)
    for block in range(4):
        load_weight(block).wait()
        both = dot(doubled, input_weight_v[block].reshape(1024, 128))
        in_part[:, :, 128 * block : 128 * block + 128] = both[:32].reshape(NR, 2, 128)
        in_part[:, :, 512 + 128 * block : 640 + 128 * block] = both[32:].reshape(NR, 2, 128)
    load("step_weight").wait()
    step_rows = jnp.concatenate(
        [step_weight_v[...].astype(F32), jnp.zeros((120, 512), F32)], axis=0
    ).astype(BF)
    in_part[:, :, 1024:1152] = dot_nt(gained, step_rows).reshape(NR, 2, 128)
    send_row(11, in_part, in_buf)
    in_buf[i] = in_part[i]

    for name in ("conv_inner_weight", "conv_group_weight", "conv_inner_state", "conv_group_state"):
        load(name).wait()
    arrived(0, group_buf)
    group_new = jnp.sum(group_buf[...], axis=0).astype(BF)
    group_old = conv_group_state_v[...].astype(F32)
    group_taps = conv_group_weight_v[...].astype(F32)
    group_mix = (
        group_old[0] * group_taps[0:1]
        + group_old[1] * group_taps[1:2]
        + group_old[2] * group_taps[2:3]
        + group_new.astype(F32) * group_taps[3:4]
    )
    pair_buf[j] = silu(group_mix).astype(BF)
    send_head(1, None, pair_buf)
    lend_lexicon.start()

    next_conv_group[0] = conv_group_state_v[1]
    next_conv_group[1] = conv_group_state_v[2]
    next_conv_group[2] = group_new
    arrived(11, in_buf)
    projected = jnp.sum(in_buf[...], axis=0)
    inner_new = projected[:, 512:1024].astype(BF)
    next_conv_inner[0] = conv_inner_state_v[1]
    next_conv_inner[1] = conv_inner_state_v[2]
    next_conv_inner[2] = inner_new
    inner_old = conv_inner_state_v[...].astype(F32)
    inner_taps = conv_inner_weight_v[...].astype(F32)
    conv_inner = silu(
        inner_old[0] * inner_taps[0:1]
        + inner_old[1] * inner_taps[1:2]
        + inner_old[2] * inner_taps[2:3]
        + inner_new.astype(F32) * inner_taps[3:4]
    )
    gate = silu(projected[:, :512])
    step_raw = projected[:, 1024:1032]
    saves = [
        save(1, next_conv_inner, next_conv_inner_h),
        save(2, next_conv_group, next_conv_group_h),
    ]
    for name in ("timestep_bias", "decay_log", "skip_gain"):
        load(name).wait()
    head_of = iota((2, 512), 1) // HEAD_DIM
    step_in = jnp.zeros((2, 512), F32)
    rate_log = jnp.zeros((2, 512), F32)
    skip = jnp.zeros((2, 512), F32)
    for h in range(8):
        here = head_of == h
        step_in = jnp.where(here, step_raw[:, h : h + 1] + timestep_bias[h], step_in)
        rate_log = jnp.where(here, decay_log[h], rate_log)
        skip = jnp.where(here, skip_gain[h], skip)
    step_size = jnp.maximum(step_in, 0.0) + jnp.log1p(jnp.exp(-jnp.abs(step_in)))
    decay = jnp.exp(-step_size * jnp.exp(rate_log))
    driven = step_size * conv_inner

    group_at = j // (NH // GROUPS)
    channel_at, entry_at = iota((128, 256), 0), iota((128, 256), 1)
    pick = (channel_at == (entry_at % 16) * GROUPS + group_at).astype(F32).astype(BF)
    source_at, entry_of = iota((NH, 256), 0), iota((NH, 256), 1) // 16
    load("mixer_gain").wait()
    arrived(1, pair_buf)
    inputs, readouts = [], []
    for r in range(2):
        picked = dot(pair_buf[:, r, :], pick)
        inputs.append(
            jnp.sum(jnp.where(source_at == entry_of, picked, 0.0), axis=0, keepdims=True)
        )
        readouts.append(
            jnp.sum(jnp.where(source_at == entry_of + 16, picked, 0.0), axis=0, keepdims=True)
        )
    readout = []
    for r in range(2):
        old_read = dot(readouts[r].astype(BF), state_turned[r])
        pair_dot = jnp.sum(inputs[r] * readouts[r], axis=1, keepdims=True)
        readout.append(
            decay[r : r + 1] * old_read
            + driven[r : r + 1] * pair_dot
            + skip[r : r + 1] * conv_inner[r : r + 1]
        )
    gated = jnp.concatenate(readout, axis=0) * gate
    gated_squares = jnp.sum(gated * gated, axis=1, keepdims=True)
    mixer_gain_wide = mixer_gain_v[...].astype(F32).reshape(1, 512)
    mixer_buf[i, :, 0:512] = gated
    mixer_buf[i, :, 512:640] = jnp.broadcast_to(gated_squares, (2, 128))
    share_mine[...] = jnp.broadcast_to(gated_squares, (2, 128))
    send_row(2, None, mixer_buf)
    send_across(9, share_mine, share_buf)

    rows8 = jnp.concatenate([driven, decay, jnp.zeros((4, 512), F32)], axis=0)
    columns = rows8.T
    for r in range(2):
        for h in range(8):
            at = slice(64 * h, 64 * h + 64)
            fresh = (
                columns[at, 2 + r : 3 + r] * recurrent_state_v[r, h].astype(F32)
                + columns[at, r : r + 1] * inputs[r]
            )
            next_state_v[r, h] = fresh.astype(BF)
    saves.append(save(0, next_state_v, next_state_h))

    load("output_weight").wait()
    arrived(2, mixer_buf)
    rest = share_buf.at[pl.ds(0, 3 * NR)]
    pltpu.make_async_copy(rest, rest, recv_sem.at[9]).wait()
    group_total = mixer_buf[:, :, 512:640]
    for at in range(4):
        group_total += share_buf[NR * at : NR * at + NR]
    group_scale = lax.rsqrt(group_total / (HEADS * HEAD_DIM // GROUPS) + EPSILON)[:, :, 0:1]
    mixer_rows = (mixer_buf[:, :, 0:512] * group_scale * mixer_gain_wide).astype(BF)
    mixer_rows = mixer_rows.reshape(ROWS, 512)
    mixed_part[:, 0, :] = dot(mixer_rows, output_weight_v[...])
    send_head(3, mixed_part, mixed_buf)
    mixed_buf[j] = mixed_part[j]

    load("final_gain").wait()
    final_gain_wide = final_gain_v[...].astype(F32).reshape(1, 512)
    arrived(3, mixed_buf)
    mixed = jnp.sum(mixed_buf[...], axis=0)
    out_mine = (hidden_rows[j] + mixed).astype(BF).astype(F32)
    scale_buf[i] = jnp.broadcast_to(jnp.sum(out_mine * out_mine, axis=1, keepdims=True), (1, 128))
    send_row(10, None, scale_buf)
    out_buf[j] = out_mine
    send_head(4, None, out_buf)
    arrived(10, scale_buf)
    norm_buf[j] = lax.rsqrt(jnp.sum(scale_buf[...], axis=0) / D + EPSILON)
    send_head(5, None, norm_buf)

    load("lexicon_matrix").wait()
    load("token_mask").wait()
    load("min_share").wait()
    arrived(4, out_buf)
    out_wide = out_buf[:, 0, :]
    scaled = out_wide * final_gain_wide
    upper = scaled.astype(BF)
    lower = (scaled - upper.astype(F32)).astype(BF)
    exact_mine[0:ROWS] = upper
    exact_mine[ROWS:] = lower
    lend_rows = to_sibling(15, exact_mine, exact_lent)
    lend_rows.start()
    both = dot(exact_mine[...], lexicon_v[...])
    lend_lexicon.wait()
    lend_rows.wait()
    both += dot(exact_lent[...], lexicon_lent[...])
    main = both[:ROWS] + both[ROWS:]
    coarse = main.astype(BF)
    logit_part[...] = coarse.reshape(NR, 2, 1024)
    send_half(12, logit_part, logit_buf)
    logit_buf[half_slot] = logit_part[i]
    main_rest = main - coarse.astype(F32)
    scaled_lent = exact_lent[0:ROWS].astype(F32) + exact_lent[ROWS:].astype(F32)
    layer_out[...] = out_wide.astype(BF)
    saves.append(save(3, layer_out, layer_out_h))

    arrived(5, norm_buf)
    row_scale = norm_buf[:, 0, :][:, 0:1]

    def rounding(product):
        exact = product * row_scale
        return (exact.astype(BF).astype(F32) - exact).astype(BF)

    rest = dot(rounding(scaled), lexicon_v[...]) + dot(rounding(scaled_lent), lexicon_lent[...])
    rest_part[...] = (rest + main_rest * row_scale).astype(BF).reshape(NR, 2, 1024)
    send_half(13, rest_part, rest_buf)
    rest_buf[half_slot] = rest_part[i]
    scale_mine = jnp.concatenate([norm_buf[2 * i], norm_buf[2 * i + 1]], axis=0)[:, 0:1]

    allowed = token_mask_v[...] > 0
    row_at = iota((2, 1), 0)
    floor_share = (
        jnp.where(row_at == 0, min_share[0], min_share[1]).astype(F32) / FIXED_POINT
    )

    def half_sums(buf):
        return jnp.concatenate(
            [
                jnp.sum(buf[0:8].astype(F32), axis=0),
                jnp.sum(buf[8:16].astype(F32), axis=0),
            ],
            axis=1,
        )

    arrived(12, logit_buf)
    main_sum = half_sums(logit_buf) * scale_mine
    arrived(13, rest_buf)
    scores = (main_sum + half_sums(rest_buf)) * INVERSE_HEAT
    peak_mine = jnp.max(jnp.where(allowed, scores, NEG_LARGE), axis=1, keepdims=True)
    peak_buf[j] = jnp.broadcast_to(peak_mine, (2, 128))
    send_head(6, None, peak_buf)
    arrived(6, peak_buf)
    peak = jnp.max(peak_buf[...], axis=0)[:, 0:1]
    ratio = jnp.where(allowed, jnp.exp(scores - peak), 0.0)
    weights = ratio * jnp.clip(ratio / floor_share - 1.0, 0.0, 1.0)
    total_mine = jnp.sum(weights, axis=1, keepdims=True)
    total_buf[j] = jnp.broadcast_to(total_mine, (2, 128))
    send_head(7, None, total_buf)
    arrived(7, total_buf)
    total = jnp.sum(total_buf[...], axis=0)[:, 0:1]
    next_probs[...] = (weights / total).astype(BF)

    saves.append(save(4, next_probs, next_probs_h))
    for copy in saves:
        copy.wait()
    for phase, dst in enumerate(
        (
            group_buf,
            pair_buf,
            mixer_buf,
            mixed_buf,
            out_buf,
            norm_buf,
            peak_buf,
            total_buf,
            square_buf,
            share_buf.at[pl.ds(0, 3 * NR + 1)],
            scale_buf,
            in_buf,
            logit_buf,
            rest_buf,
        )
    ):
        sent(phase, dst)


def finish(*refs):
    sems = refs[-1]
    copies = [
        pltpu.make_async_copy(refs[at], refs[at + 5], sems.at[at]) for at in range(5)
    ]
    for copy in copies:
        copy.start()
    for copy in copies:
        copy.wait()


def local(
    hidden,
    norm_gain,
    input_weight,
    group_weight,
    step_weight,
    conv_inner_weight,
    conv_group_weight,
    conv_inner_state,
    conv_group_state,
    timestep_bias,
    decay_log,
    skip_gain,
    recurrent_state,
    mixer_gain,
    output_weight,
    final_gain,
    lexicon_matrix,
    token_mask,
    min_share,
):
    hbm = pl.BlockSpec(memory_space=pltpu.HBM)
    in_specs = [hbm] * N_IN
    shapes = (
            jax.ShapeDtypeStruct((2, 8, 64, 256), BF),
            jax.ShapeDtypeStruct((3, 2, 512), BF),
            jax.ShapeDtypeStruct((3, 2, 128), BF),
            jax.ShapeDtypeStruct((ROWS, 512), BF),
            jax.ShapeDtypeStruct((2, 2048), BF),
    )
    results = pl.pallas_call(
        kernel,
        out_shape=tuple(pltpu.VMEM(shape.shape, BF) for shape in shapes),
        in_specs=in_specs,
        out_specs=(pl.BlockSpec(memory_space=pltpu.VMEM),) * 5,
        scratch_shapes=[
            pltpu.VMEM((ROWS, 512), BF),
            pltpu.VMEM((512,), BF),
            pltpu.VMEM((4, 512, 2, 128), BF),
            pltpu.VMEM((512, 128), BF),
            pltpu.VMEM((8, 512), BF),
            pltpu.VMEM((4, 512), BF),
            pltpu.VMEM((4, 128), BF),
            pltpu.VMEM((3, 2, 512), BF),
            pltpu.VMEM((3, 2, 128), BF),
            pltpu.VMEM((2, 8, 64, 256), BF),
            pltpu.VMEM((512,), BF),
            pltpu.VMEM((512, 512), BF),
            pltpu.VMEM((512,), BF),
            pltpu.VMEM((512, 1024), BF),
            pltpu.VMEM((2, 2048), jnp.int32),
            pltpu.VMEM((2, 8, 64, 256), BF),
            pltpu.VMEM((3, 2, 512), BF),
            pltpu.VMEM((3, 2, 128), BF),
            pltpu.VMEM((ROWS, 512), BF),
            pltpu.VMEM((2, 2048), BF),
            pltpu.SMEM((8,), F32),
            pltpu.SMEM((8,), F32),
            pltpu.SMEM((8,), F32),
            pltpu.SMEM((2,), jnp.int32),
            pltpu.VMEM((2, 256, 512), BF),
            pltpu.VMEM((ROWS, 1, 512), F32),
            pltpu.VMEM((NR, 1, 128), F32),
            pltpu.VMEM((NR, 2, 128), F32),
            pltpu.VMEM((NR, 2, 128), F32),
            pltpu.VMEM((NR, 2, 1152), F32),
            pltpu.VMEM((NR, 2, 1152), F32),
            pltpu.VMEM((NH, 2, 128), BF),
            pltpu.VMEM((2, 128), F32),
            pltpu.VMEM((4 * NR, 2, 128), F32),
            pltpu.VMEM((NR, 2, 640), F32),
            pltpu.VMEM((ROWS, 1, 512), F32),
            pltpu.VMEM((NH, 1, 512), F32),
            pltpu.VMEM((NR, 1, 128), F32),
            pltpu.VMEM((NH, 1, 512), F32),
            pltpu.VMEM((NH, 1, 128), F32),
            pltpu.VMEM((NR, 2, 1024), BF),
            pltpu.VMEM((NR, 2, 1024), BF),
            pltpu.VMEM((NR, 2, 1024), BF),
            pltpu.VMEM((NR, 2, 1024), BF),
            pltpu.VMEM((512, 1024), BF),
            pltpu.VMEM((2 * ROWS, 512), BF),
            pltpu.VMEM((2 * ROWS, 512), BF),
            pltpu.VMEM((NH, 2, 128), F32),
            pltpu.VMEM((NH, 2, 128), F32),
            pltpu.SemaphoreType.DMA((len(SMALL),)),
            pltpu.SemaphoreType.DMA((4,)),
            pltpu.SemaphoreType.DMA((5,)),
            pltpu.SemaphoreType.DMA((16,)),
            pltpu.SemaphoreType.DMA((16,)),
            pltpu.SemaphoreType.REGULAR,
        ],
        compiler_params=pltpu.CompilerParams(
            collective_id=0, has_side_effects=True, vmem_limit_bytes=56 << 20
        ),
    )(
        hidden,
        norm_gain,
        input_weight,
        group_weight,
        step_weight.T,
        conv_inner_weight,
        conv_group_weight,
        jnp.transpose(conv_inner_state, (1, 0, 2)),
        jnp.transpose(conv_group_state, (1, 0, 2)),
        timestep_bias,
        decay_log,
        skip_gain,
        recurrent_state,
        mixer_gain,
        output_weight,
        final_gain,
        lexicon_matrix,
        token_mask,
        min_share,
    )
    state, inner, group, out, probs = pl.pallas_call(
        finish,
        out_shape=shapes,
        in_specs=[pl.BlockSpec(memory_space=pltpu.VMEM)] * 5,
        out_specs=[hbm] * 5,
        scratch_shapes=[pltpu.SemaphoreType.DMA((5,))],
        compiler_params=pltpu.CompilerParams(vmem_limit_bytes=1 << 20),
    )(*results)
    return (
        state,
        jnp.transpose(inner, (1, 0, 2)),
        jnp.transpose(group, (1, 0, 2)),
        out,
        probs,
    )


def solution(mesh):
    in_specs = (
        P(None, "row"),
        P("row"),
        P("row", None, "head"),
        P("row", "head"),
        P("row", "head"),
        P(None, "head"),
        P(None, "head"),
        P("row", None, "head"),
        P("row", None, "head"),
        P("head"),
        P("head"),
        P("head"),
        P("row", "head", None, None),
        P("head"),
        P("head", "row"),
        P("row"),
        P("row", "head"),
        P("row", "head"),
        P("row"),
    )
    out_specs = (
        P("row", "head", None, None),
        P("row", None, "head"),
        P("row", None, "head"),
        P(None, "row"),
        P("row", "head"),
    )
    return jax.shard_map(local, mesh=mesh, in_specs=in_specs, out_specs=out_specs, check_vma=False)
```
